128 devices in a mesh: wide: 32 (over y, x, core), narrow: 4 (over z).
Axes of the slice: x: 4, y: 4, z: 4, core: 2. Of those that a mesh axis runs over, the one named last changes fastest.
Arguments:
- node_feats: bfloat16 [32768, 512], P(('wide', 'narrow')), may hold values from -6 to 6
- halo_rows: int32 [32, 4, 32, 16], P('wide', 'narrow'), may hold values from 0 to 255
- edge_src: int32 [256, 2048], P(('wide', 'narrow')), may hold values from 0 to 3071, as said below
- edge_dst: int32 [256, 2048], P(('wide', 'narrow')), may hold values from 0 to 128, as said below
- dest_weight: bfloat16 [512, 1024], replicated, may hold values from -0.25 to 0.25
- source_weight: bfloat16 [512, 1024], replicated, may hold values from -0.25 to 0.25
- norm_gain: float32 [512], replicated, may hold values from 0.1 to 1.9
- router_weight: bfloat16 [512, 64], replicated, may hold values from -0.25 to 0.25
- routes: int32 [32768, 2], P(('wide', 'narrow')), may hold values from 0 to 63, all different within a row; in each aligned block of 256 rows (0 to 255, 256 to 511, ...) at most 16 rows name the same one
- expert_in: bfloat16 [64, 512, 1024], P('wide', None, 'narrow'), may hold values from -0.25 to 0.25
- expert_out: bfloat16 [64, 1024, 512], P('wide', 'narrow'), may hold values from -0.1875 to 0.1875
- cotangent: bfloat16 [32768, 512], P(('wide', 'narrow')), may hold values from -0.75 to 0.75
Outputs:
- layer_out: bfloat16 [32768, 512], P(('wide', 'narrow'))
- grad_features: float32 [32768, 512], P(('wide', 'narrow'))
- grad_expert_in: float32 [64, 512, 1024], P('wide', None, 'narrow')
- grad_expert_out: float32 [64, 1024, 512], P('wide', 'narrow')
- grad_router: float32 [512, 64], replicated
The draws below stay inside these ranges and needn't reach their ends.
Inputs may be any that keep to these rules, and one draw needn't show every extreme that they name: `routes`: the rows of one device name any one expert at most 16 times, a bound that some block reaches. `edge_dst`: 128 marks an empty slot; in each tile the live slots come first; every device has a tile whose 2048 slots are all live. `edge_src`: A row of the src_table of the device that holds the tile.
All inputs are finite; a program needn't handle non-finite values.
Results may differ from the reference program's by a relative error of at most 0.019.
Values may be sent and summed in bfloat16 or wider, within the bound.
No kernel may reach another device: no remote copies, remote signals or barrier semaphores. Data moves between devices by JAX's collectives and lax.ppermute only.
A program may use at most 128 MiB of HBM per device.

```python
import math
import jax
import jax.numpy as jnp
import numpy as np
from jax import lax

D = 512
FF = 1024
TILE = 128
EDGE_TILE = 2048
HALO_PEER = 16
ROWS_DEV = 256
EXPERTS = 64
CAP = 16
TILES_DEV = 2
NODES = 32768
TILES = 256
SRC_ROWS = 3072
N_WIDE = 32
N_NARROW = 4


def edge_pair(key):
    subkeys = jax.random.split(jax.random.fold_in(key, 11), 4)
    counts = jax.random.randint(subkeys[0], (TILES,), EDGE_TILE // 2, EDGE_TILE + 1)
    chosen = jax.random.randint(subkeys[1], (TILES // TILES_DEV,), 0, TILES_DEV)
    full_tile = jnp.arange(TILES) % TILES_DEV == jnp.repeat(chosen, TILES_DEV)
    counts = jnp.where(full_tile, EDGE_TILE, counts)
    live_mask = jnp.arange(EDGE_TILE)[None, :] < counts[:, None]
    targets = jnp.where(live_mask, jax.random.randint(subkeys[2], (TILES, EDGE_TILE), 0, TILE), TILE)
    sources = jax.random.randint(subkeys[3], (TILES, EDGE_TILE), 0, SRC_ROWS)
    return (sources.astype(jnp.int32), targets.astype(jnp.int32))


def draw_edge_src(key, part):
    return edge_pair(key)[0]


def draw_edge_dst(key, part):
    return edge_pair(key)[1]


def touch_ends(entries, rng, least, top_value):
    shape = entries.shape
    spot = [jax.random.randint(jax.random.fold_in(rng, axis), (), 0, shape[axis]) for axis in range(len(shape))]
    entries = entries.at[tuple(spot)].set(least)
    longest = shape.index(max(shape))
    spot[longest] = (spot[longest] + 1) % shape[longest]
    return entries.at[tuple(spot)].set(top_value)


def shard_levels(stream_key, dims, cuts, smallest, top_value):
    gain, own = 1.0, jax.random.fold_in(stream_key, 6)
    for dim, shards_of in cuts:
        heights = jnp.exp(jax.random.uniform(jax.random.fold_in(own, dim), (shards_of,), jnp.float32, smallest / len(cuts), top_value / len(cuts)))
        gain = gain * jnp.repeat(heights, dims[dim] // shards_of).reshape([-1 if axis == dim else 1 for axis in range(len(dims))])
    return gain


def deal_out(rng, own, number, rows, number_of, top, bound, skew):
    ranking = jax.random.permutation(rng, number_of)
    heavy_load, ordinary = portions_of(number_of, rows * top, bound, skew, True), portions_of(number_of, rows * top, bound, skew, False)
    places = jnp.arange(number_of)

    def named(lengths, offset_by):
        used = int((lengths > 0).sum())
        fixed = max(1, used // 4)
        passed = fixed + (places - fixed + offset_by * (used - fixed)) % max(1, number_of - fixed)
        return jnp.zeros((number_of,), jnp.int32).at[ranking[jnp.where(places < fixed, places, passed)]].set(jnp.asarray(lengths, jnp.int32))

    lengths = jnp.where(number % 4 == 0, named(heavy_load, number // 4), named(ordinary, number - number // 4 - 1))
    mixed = jax.random.permutation(jax.random.fold_in(own, 3), number_of)
    giver, receiver = mixed[0:number_of // 2 * 2:2], mixed[1:number_of // 2 * 2:2]
    margin = jnp.minimum(lengths[giver] - 1, bound - lengths[receiver]) // 2
    margin = jnp.where((giver == ranking[0]) | (receiver == ranking[0]) | (lengths[receiver] == 0), 0, jnp.maximum(margin, 0))
    passed = jax.random.randint(jax.random.fold_in(own, 4), (number_of // 2,), 0, 1 << 20) % (margin + 1)
    lengths = lengths.at[giver].add(-passed).at[receiver].add(passed)
    members = jnp.searchsorted(jnp.cumsum(lengths), jnp.arange(rows * top), side="right").astype(jnp.int32)
    table = members.reshape(top, rows).T
    table = table[jax.random.permutation(jax.random.fold_in(own, 1), rows)]
    offset_by = jax.random.randint(jax.random.fold_in(own, 2), (rows, 1), 0, top)
    return jnp.take_along_axis(table, (jnp.arange(top)[None, :] + offset_by) % top, axis=1)


def portions_of(count, total, most, slope, full):
    loads = [(1 << 20) // math.isqrt(rank ** slope) + 1 for rank in range(1, count + 1)]
    largest = most if full else min(most, max(-(-total // count), total * loads[0] // sum(loads)))
    least = 1 if total - largest >= count - 1 else 0
    given, surplus = [largest] + [least] * (count - 1), total - largest - least * (count - 1)
    while surplus > 0:
        candidates = [i for i in range(1, count) if given[i] < largest] or [i for i in range(1, count) if given[i] < most]
        whole, left = sum([loads[i] for i in candidates]), surplus
        for i in candidates:
            extra = min(most - given[i], max(1, left * loads[i] // whole), surplus)
            given[i] = given[i] + extra
            surplus = surplus - extra
    return np.array(given)


def gaussian(rng, dims, scale, most, pieces=(), kind=jnp.bfloat16):
    result = jax.random.normal(rng, dims, jnp.float32) * scale
    if len(pieces) > 0:
        result = shard_levels(rng, dims, pieces, -0.22, 0.18) * result
    return jnp.clip(result, min=-most, max=most).astype(kind)


def setup_inputs(seed: int = 0) -> dict:
    key_list = jax.random.split(jax.random.key(seed), 13)
    node_feats = gaussian(key_list[0], (NODES, D), 1.0, 6.0, ((0, 128),))
    halo_rows = touch_ends(jax.random.randint(key_list[1], (N_WIDE, N_NARROW, N_WIDE, HALO_PEER), 0, ROWS_DEV), jax.random.fold_in(key_list[1], 1), 0, ROWS_DEV - 1).astype(jnp.int32)
    edge_src = draw_edge_src(jax.random.fold_in(key_list[12], 71), 0)
    edge_dst = draw_edge_dst(jax.random.fold_in(key_list[12], 71), 0)
    dest_weight = gaussian(key_list[4], (D, 2 * D), D ** -0.5, 0.25)
    source_weight = gaussian(key_list[5], (D, 2 * D), D ** -0.5, 0.25)
    norm_gain = jnp.clip(1.0 + 0.18 * jax.random.normal(key_list[6], (D,), jnp.float32), 0.1, 1.9)
    router_weight = gaussian(key_list[7], (D, EXPERTS), D ** -0.5, 0.25)
    routes_keys = jax.random.split(jax.random.fold_in(key_list[8], 1), NODES // ROWS_DEV)
    routes_turns = jax.random.permutation(jax.random.fold_in(key_list[8], 3), NODES // ROWS_DEV)
    routes = jax.vmap(lambda own, number: deal_out(jax.random.fold_in(key_list[8], 2), own, number, ROWS_DEV, EXPERTS, 2, CAP, 2))(routes_keys, routes_turns).reshape((NODES, 2))
    expert_in = gaussian(key_list[9], (EXPERTS, D, FF), D ** -0.5, 0.25, ((0, 32), (2, 4)))
    expert_out = gaussian(key_list[10], (EXPERTS, FF, D), FF ** -0.5, 0.1875, ((0, 32), (1, 4)))
    cotangent = gaussian(key_list[11], (NODES, D), 0.125, 0.75, ((0, 128),))
    return dict(node_feats=node_feats, halo_rows=halo_rows, edge_src=edge_src, edge_dst=edge_dst, dest_weight=dest_weight, source_weight=source_weight, norm_gain=norm_gain, router_weight=router_weight, routes=routes, expert_in=expert_in, expert_out=expert_out, cotangent=cotangent)


def tile_sums(src_table, sources, targets, dest_part):
    feat_width = dest_part.shape[1]
    picked = jnp.take(src_table, sources, axis=0)
    source_gate = picked[:, :feat_width].astype(jnp.float32)
    source_value = picked[:, feat_width:].astype(jnp.float32)
    dest_gate = jnp.take(dest_part, jnp.minimum(targets, TILE - 1), axis=0)
    gate_vals = jax.nn.sigmoid(dest_gate + source_gate).astype(jnp.bfloat16)
    messages = (gate_vals.astype(jnp.float32) * source_value).astype(jnp.bfloat16)
    selector = (targets[None, :] == jnp.arange(TILE, dtype=jnp.int32)[:, None]).astype(jnp.bfloat16)
    totals = jnp.dot(selector, jnp.concatenate([messages, gate_vals], axis=1), preferred_element_type=jnp.float32)
    return totals[:, :feat_width] / jnp.maximum(totals[:, feat_width:], 1.0)

def graph_update(node_feats, dest_proj, agg, norm_gain):
    feat_width = node_feats.shape[1]
    pre_norm = dest_proj[:, feat_width:] + agg
    average = lax.optimization_barrier(jnp.mean(pre_norm, axis=1, keepdims=True))
    center = pre_norm - average
    variance = lax.optimization_barrier(jnp.mean(center * center, axis=1, keepdims=True))
    normed = center * lax.rsqrt(variance + 1e-05) * norm_gain
    return (node_feats.astype(jnp.float32) + jax.nn.relu(normed)).astype(jnp.bfloat16)

def reference(node_feats, halo_rows, edge_src, edge_dst, dest_weight, source_weight, norm_gain, router_weight, routes, expert_in, expert_out, cotangent):
    src_proj = jnp.dot(node_feats, source_weight, preferred_element_type=jnp.float32).astype(jnp.bfloat16)
    dest_proj = jnp.dot(node_feats, dest_weight, preferred_element_type=jnp.float32)
    proj_blocks = src_proj.reshape(N_WIDE, N_NARROW, ROWS_DEV, 2 * D)
    dest_gates = dest_proj[:, :D].reshape(N_WIDE, N_NARROW * TILES_DEV, TILE, D)
    src_tiles = edge_src.reshape(N_WIDE, N_NARROW * TILES_DEV, EDGE_TILE)
    dst_tiles = edge_dst.reshape(N_WIDE, N_NARROW * TILES_DEV, EDGE_TILE)
    wide_ids = jnp.arange(N_WIDE, dtype=jnp.int32)
    narrow_ids = jnp.arange(N_NARROW, dtype=jnp.int32)

    def partition_agg(part_items):
        wide_index, sources, targets, gates_part = part_items
        chosen = lax.dynamic_index_in_dim(halo_rows, wide_index, axis=2, keepdims=False)
        halo_part = proj_blocks[wide_ids[:, None, None], narrow_ids[None, :, None], chosen]
        halo_part = jnp.transpose(halo_part, (1, 0, 2, 3)).reshape(-1, 2 * D)
        own_part = lax.dynamic_index_in_dim(proj_blocks, wide_index, axis=0, keepdims=False).reshape(-1, 2 * D)
        src_table = jnp.concatenate([own_part, halo_part], axis=0)
        return lax.map(lambda tile_items: tile_sums(src_table, tile_items[0], tile_items[1], tile_items[2]), (sources, targets, gates_part))
    agg = lax.map(partition_agg, (wide_ids, src_tiles, dst_tiles, dest_gates)).reshape(NODES, D)
    graph_out = graph_update(node_feats, dest_proj, agg, norm_gain)
    logits = jnp.dot(graph_out, router_weight, preferred_element_type=jnp.float32)
    route_first = routes[:, 0]
    route_second = routes[:, 1]
    logit_first = jnp.take_along_axis(logits, route_first[:, None], axis=1)[:, 0]
    logit_second = jnp.take_along_axis(logits, route_second[:, None], axis=1)[:, 0]
    weight_first = jax.nn.sigmoid(logit_first - logit_second)
    weight_second = 1.0 - weight_first
    combine = jnp.stack([weight_first, weight_second], axis=1)
    expert_grads = (combine[:, :, None] * cotangent.astype(jnp.float32)[:, None, :]).astype(jnp.bfloat16).reshape(2 * NODES, D)
    device_count = N_WIDE * N_NARROW
    routes_dev = routes.reshape(device_count, 2 * ROWS_DEV)
    expert_hits = (routes_dev[:, :, None] == jnp.arange(EXPERTS, dtype=jnp.int32)[None, None, :]).astype(jnp.int32)
    position = lax.optimization_barrier(jnp.sum((jnp.cumsum(expert_hits, axis=1) - 1) * expert_hits, axis=2))
    dev_ids = jnp.arange(device_count, dtype=jnp.int32)[:, None]
    global_ids = dev_ids * (2 * ROWS_DEV) + jnp.arange(2 * ROWS_DEV, dtype=jnp.int32)[None, :]
    owner_ids = jnp.full((EXPERTS, N_NARROW, N_WIDE, CAP), 2 * NODES, jnp.int32)
    owner_ids = owner_ids.at[routes_dev, dev_ids % N_NARROW, dev_ids // N_NARROW, position].set(global_ids)
    rows_twice = jnp.concatenate([jnp.repeat(graph_out, 2, axis=0), jnp.zeros((1, D), jnp.bfloat16)], axis=0)
    grads_twice = jnp.concatenate([expert_grads, jnp.zeros((1, D), jnp.bfloat16)], axis=0)

    def expert_step(carry, step_items):
        out_all, back_all = carry
        owned_ids, weight_in, weight_out = step_items
        flat_owned = owned_ids.reshape(-1)
        rows_in = jnp.take(rows_twice, flat_owned, axis=0)
        grads_in = jnp.take(grads_twice, flat_owned, axis=0)
        hidden = jnp.dot(rows_in, weight_in, preferred_element_type=jnp.float32)
        activated, gelu_back = jax.vjp(jax.nn.gelu, hidden)
        act_low = activated.astype(jnp.bfloat16)
        outputs = jnp.dot(act_low, weight_out, preferred_element_type=jnp.float32).astype(jnp.bfloat16)
        act_grad = jnp.dot(grads_in, weight_out.T, preferred_element_type=jnp.float32)
        hidden_grad = gelu_back(act_grad)[0].astype(jnp.bfloat16)
        grad_rows = jnp.dot(hidden_grad, weight_in.T, preferred_element_type=jnp.float32).astype(jnp.bfloat16)
        rows_split = rows_in.reshape(N_NARROW, -1, D).astype(jnp.float32)
        hidden_split = hidden_grad.reshape(N_NARROW, -1, FF).astype(jnp.float32)
        act_split = act_low.reshape(N_NARROW, -1, FF).astype(jnp.float32)
        grads_split = grads_in.reshape(N_NARROW, -1, D).astype(jnp.float32)
        grad_w_in = jnp.einsum('nrd,nrh->ndh', rows_split, hidden_split, precision=lax.Precision.HIGHEST)
        grad_w_out = jnp.einsum('nrh,nrd->nhd', act_split, grads_split, precision=lax.Precision.HIGHEST)
        grad_w_in = lax.optimization_barrier(jnp.sum(lax.optimization_barrier(grad_w_in.astype(jnp.bfloat16)).astype(jnp.float32), axis=0))
        grad_w_out = lax.optimization_barrier(jnp.sum(lax.optimization_barrier(grad_w_out.astype(jnp.bfloat16)).astype(jnp.float32), axis=0))
        out_all = out_all.at[flat_owned].set(outputs, mode='drop')
        back_all = back_all.at[flat_owned].set(grad_rows, mode='drop')
        return ((out_all, back_all), (grad_w_in, grad_w_out))
    initial = (jnp.zeros((2 * NODES, D), jnp.bfloat16), jnp.zeros((2 * NODES, D), jnp.bfloat16))
    (expert_y, expert_dx), (grad_expert_in, grad_expert_out) = lax.scan(expert_step, initial, (owner_ids, expert_in, expert_out))
    expert_y = expert_y.reshape(NODES, 2, D).astype(jnp.float32)
    expert_dx = expert_dx.reshape(NODES, 2, D).astype(jnp.float32)
    cot_float = cotangent.astype(jnp.float32)
    layer_out = (graph_out.astype(jnp.float32) + lax.optimization_barrier(jnp.sum(combine[:, :, None] * expert_y, axis=1))).astype(jnp.bfloat16)
    cot_dots = lax.optimization_barrier(jnp.sum(cot_float[:, None, :] * expert_y, axis=2))
    gap_grad = (cot_dots[:, 0] - cot_dots[:, 1]) * weight_first * weight_second
    router_cols = router_weight.astype(jnp.float32).T
    spread = jnp.take(router_cols, route_first, axis=0) - jnp.take(router_cols, route_second, axis=0)
    grad_features = cot_float + lax.optimization_barrier(jnp.sum(combine[:, :, None] * expert_dx, axis=1)) + gap_grad[:, None] * spread
    expert_range = jnp.arange(EXPERTS, dtype=jnp.int32)[None, :]
    dlogits = gap_grad[:, None] * ((route_first[:, None] == expert_range).astype(jnp.float32) - (route_second[:, None] == expert_range).astype(jnp.float32))
    grad_router = jnp.dot(graph_out.astype(jnp.float32).T, dlogits, precision=lax.Precision.HIGHEST)
    return (layer_out, grad_features, grad_expert_in, grad_expert_out, grad_router)
```

```python
import jax
import jax.numpy as jnp
from jax import lax
from jax.sharding import PartitionSpec as P

TILE = 128


def tile_sums(src_table, sources, targets, dest_part):
    feat_width = dest_part.shape[1]
    picked = jnp.take(src_table, sources, axis=0)
    source_gate = picked[:, :feat_width].astype(jnp.float32)
    source_value = picked[:, feat_width:].astype(jnp.float32)
    dest_gate = jnp.take(dest_part, jnp.minimum(targets, TILE - 1), axis=0)
    gate_vals = jax.nn.sigmoid(dest_gate + source_gate).astype(jnp.bfloat16)
    messages = (gate_vals.astype(jnp.float32) * source_value).astype(jnp.bfloat16)
    selector = (targets[None, :] == jnp.arange(TILE, dtype=jnp.int32)[:, None]).astype(jnp.bfloat16)
    totals = jnp.dot(
        selector, jnp.concatenate([messages, gate_vals], axis=1), preferred_element_type=jnp.float32
    )
    return totals[:, :feat_width] / jnp.maximum(totals[:, feat_width:], 1.0)


def graph_update(node_feats, dest_proj, agg, norm_gain):
    feat_width = node_feats.shape[1]
    pre_norm = dest_proj[:, feat_width:] + agg
    average = jnp.mean(pre_norm, axis=1, keepdims=True)
    center = pre_norm - average
    variance = jnp.mean(center * center, axis=1, keepdims=True)
    normed = center * lax.rsqrt(variance + 1e-05) * norm_gain
    return (node_feats.astype(jnp.float32) + jax.nn.relu(normed)).astype(jnp.bfloat16)


def expert_block(rows_in, grads_in, weight_in, weight_out):
    hidden = jnp.einsum("erd,edh->erh", rows_in, weight_in, preferred_element_type=jnp.float32)
    activated, gelu_back = jax.vjp(jax.nn.gelu, hidden)
    act_low = activated.astype(jnp.bfloat16)
    outputs = jnp.einsum(
        "erh,ehd->erd", act_low, weight_out, preferred_element_type=jnp.float32
    ).astype(jnp.bfloat16)
    act_grad = jnp.einsum("erd,ehd->erh", grads_in, weight_out, preferred_element_type=jnp.float32)
    hidden_grad = gelu_back(act_grad)[0].astype(jnp.bfloat16)
    grad_rows = jnp.einsum(
        "erh,edh->erd", hidden_grad, weight_in, preferred_element_type=jnp.float32
    ).astype(jnp.bfloat16)
    grad_w_in = jnp.einsum("erd,erh->edh", rows_in, hidden_grad, preferred_element_type=jnp.float32)
    grad_w_out = jnp.einsum("erh,erd->ehd", act_low, grads_in, preferred_element_type=jnp.float32)
    return (outputs, grad_rows, grad_w_in, grad_w_out)


def on_device(
    node_feats,
    halo_rows,
    edge_src,
    edge_dst,
    dest_weight,
    source_weight,
    norm_gain,
    router_weight,
    routes,
    expert_in,
    expert_out,
    cotangent,
):
    row_count, feat_width = node_feats.shape
    wide_count = lax.axis_size("wide")
    halo_list = halo_rows.reshape(wide_count, -1)
    dest_proj = jnp.dot(node_feats, dest_weight, preferred_element_type=jnp.float32)
    row_width = node_feats.shape[1]
    halo_send = jnp.take(node_feats, halo_list, axis=0)
    received = lax.all_to_all(halo_send, "wide", split_axis=0, concat_axis=0, tiled=True)
    partition, arrived = (
        lax.all_gather(node_feats, "narrow", axis=0, tiled=True),
        lax.all_gather(received, "narrow", axis=0, tiled=True),
    )
    src_table = jnp.concatenate([partition, arrived.reshape(-1, row_width)], axis=0)
    src_table = jnp.dot(src_table, source_weight, preferred_element_type=jnp.float32).astype(
        jnp.bfloat16
    )
    tile_count = row_count // TILE
    dest_gates = dest_proj[:, :feat_width].reshape(tile_count, TILE, feat_width)
    agg = lax.map(
        lambda tile_items: tile_sums(src_table, tile_items[0], tile_items[1], tile_items[2]),
        (edge_src, edge_dst, dest_gates),
    )
    agg = agg.reshape(row_count, feat_width)
    graph_out = graph_update(node_feats, dest_proj, agg, norm_gain)
    expert_count = router_weight.shape[1]
    logits = jnp.dot(graph_out, router_weight, preferred_element_type=jnp.float32)
    route_first = routes[:, 0]
    route_second = routes[:, 1]
    logit_first = jnp.take_along_axis(logits, route_first[:, None], axis=1)[:, 0]
    logit_second = jnp.take_along_axis(logits, route_second[:, None], axis=1)[:, 0]
    weight_first = jax.nn.sigmoid(logit_first - logit_second)
    weight_second = 1.0 - weight_first
    combine = jnp.stack([weight_first, weight_second], axis=1)
    cot_float = cotangent.astype(jnp.float32)
    expert_grads = (
        (combine[:, :, None] * cot_float[:, None, :])
        .astype(jnp.bfloat16)
        .reshape(2 * row_count, feat_width)
    )
    flat_routes = routes.reshape(-1)
    expert_hits = (
        flat_routes[:, None] == jnp.arange(expert_count, dtype=jnp.int32)[None, :]
    ).astype(jnp.bfloat16)
    slot_ids = jnp.arange(2 * row_count, dtype=jnp.int32)
    earlier = (slot_ids[None, :] < slot_ids[:, None]).astype(jnp.bfloat16)
    ahead = jnp.dot(earlier, expert_hits, preferred_element_type=jnp.float32)
    position = jnp.sum(ahead * expert_hits.astype(jnp.float32), axis=1).astype(jnp.int32)
    capacity = 4 * row_count // expert_count
    slot_index = flat_routes * capacity + position
    buffer_shape = (wide_count, expert_count // wide_count, capacity, feat_width)
    rows_twice = jnp.repeat(graph_out, 2, axis=0)
    send_rows = (
        jnp.zeros((expert_count * capacity, feat_width), jnp.bfloat16)
        .at[slot_index]
        .set(rows_twice)
        .reshape(buffer_shape)
    )
    send_grads = (
        jnp.zeros((expert_count * capacity, feat_width), jnp.bfloat16)
        .at[slot_index]
        .set(expert_grads)
        .reshape(buffer_shape)
    )
    rows_in, grads_in = (
        lax.all_to_all(send_rows, "wide", split_axis=0, concat_axis=2, tiled=True),
        lax.all_to_all(send_grads, "wide", split_axis=0, concat_axis=2, tiled=True),
    )
    weight_in, weight_out = (
        lax.all_gather(expert_in, "narrow", axis=2, tiled=True),
        lax.all_gather(expert_out, "narrow", axis=1, tiled=True),
    )
    outputs, grad_rows, grad_w_in, grad_w_out = expert_block(
        rows_in[0], grads_in[0], weight_in, weight_out
    )
    grad_expert_in, grad_expert_out = (
        lax.psum_scatter(
            grad_w_in.astype(jnp.bfloat16), "narrow", scatter_dimension=2, tiled=True
        ).astype(jnp.float32),
        lax.psum_scatter(
            grad_w_out.astype(jnp.bfloat16), "narrow", scatter_dimension=1, tiled=True
        ).astype(jnp.float32),
    )
    back_out, back_grad = (
        lax.all_to_all(outputs[None], "wide", split_axis=2, concat_axis=0, tiled=True),
        lax.all_to_all(grad_rows[None], "wide", split_axis=2, concat_axis=0, tiled=True),
    )
    expert_y = (
        jnp.take(back_out.reshape(-1, feat_width), slot_index, axis=0)
        .reshape(row_count, 2, feat_width)
        .astype(jnp.float32)
    )
    expert_dx = (
        jnp.take(back_grad.reshape(-1, feat_width), slot_index, axis=0)
        .reshape(row_count, 2, feat_width)
        .astype(jnp.float32)
    )
    layer_out = (
        graph_out.astype(jnp.float32) + jnp.sum(combine[:, :, None] * expert_y, axis=1)
    ).astype(jnp.bfloat16)
    cot_dots = jnp.sum(cot_float[:, None, :] * expert_y, axis=2)
    gap_grad = (cot_dots[:, 0] - cot_dots[:, 1]) * weight_first * weight_second
    router_cols = router_weight.astype(jnp.float32).T
    spread = jnp.take(router_cols, route_first, axis=0) - jnp.take(
        router_cols, route_second, axis=0
    )
    grad_features = (
        cot_float + jnp.sum(combine[:, :, None] * expert_dx, axis=1) + gap_grad[:, None] * spread
    )
    expert_range = jnp.arange(expert_count, dtype=jnp.int32)[None, :]
    dlogits = gap_grad[:, None] * (
        (route_first[:, None] == expert_range).astype(jnp.float32)
        - (route_second[:, None] == expert_range).astype(jnp.float32)
    )
    partial_router = jnp.dot(
        graph_out.astype(jnp.float32).T, dlogits, precision=lax.Precision.HIGHEST
    )
    grad_router = lax.psum(partial_router, ("wide", "narrow"))
    return (layer_out, grad_features, grad_expert_in, grad_expert_out, grad_router)


def solution(mesh):
    placed = (
        P(("wide", "narrow"), None),
        P("wide", "narrow", None, None),
        P(("wide", "narrow"), None),
        P(("wide", "narrow"), None),
        P(),
        P(),
        P(),
        P(),
        P(("wide", "narrow"), None),
        P("wide", None, "narrow"),
        P("wide", "narrow", None),
        P(("wide", "narrow"), None),
    )
    return jax.shard_map(
        on_device,
        mesh=mesh,
        in_specs=placed,
        out_specs=(
            P(("wide", "narrow"), None),
            P(("wide", "narrow"), None),
            P("wide", None, "narrow"),
            P("wide", "narrow", None),
            P(),
        ),
        check_vma=False,
    )
```

```python
import jax
import jax.numpy as jnp
from jax import lax
from jax.sharding import Mesh
from jax.sharding import PartitionSpec as P

TILE = 128
ALL = ("wide", "hi", "lo")
NARROW = ("hi", "lo")
OWNERS = ("wide", "lo")


def tile_sums(src_table, sources, targets, dest_part):
    feat_width = dest_part.shape[1]
    picked = jnp.take(src_table, sources, axis=0)
    source_gate = picked[:, :feat_width].astype(jnp.float32)
    source_value = picked[:, feat_width:].astype(jnp.float32)
    dest_gate = jnp.take(dest_part, jnp.minimum(targets, TILE - 1), axis=0)
    gate_vals = jax.nn.sigmoid(dest_gate + source_gate).astype(jnp.bfloat16)
    messages = (gate_vals.astype(jnp.float32) * source_value).astype(jnp.bfloat16)
    selector = (targets[None, :] == jnp.arange(TILE, dtype=jnp.int32)[:, None]).astype(jnp.bfloat16)
    totals = jnp.dot(
        selector, jnp.concatenate([messages, gate_vals], axis=1), preferred_element_type=jnp.float32
    )
    return totals[:, :feat_width] / jnp.maximum(totals[:, feat_width:], 1.0)


def graph_update(node_feats, dest_proj, agg, norm_gain):
    feat_width = node_feats.shape[1]
    pre_norm = dest_proj[:, feat_width:] + agg
    average = jnp.mean(pre_norm, axis=1, keepdims=True)
    center = pre_norm - average
    variance = jnp.mean(center * center, axis=1, keepdims=True)
    normed = center * lax.rsqrt(variance + 1e-05) * norm_gain
    return (node_feats.astype(jnp.float32) + jax.nn.relu(normed)).astype(jnp.bfloat16)


def on_device(
    node_feats,
    halo_rows,
    edge_src,
    edge_dst,
    dest_weight,
    source_weight,
    norm_gain,
    router_weight,
    routes,
    expert_in,
    expert_out,
    cotangent,
):
    row_count, feat_width = node_feats.shape
    wide_count = lax.axis_size("wide")
    narrow_count = lax.axis_size("hi") * lax.axis_size("lo")
    device_count = wide_count * narrow_count
    halo_peer = halo_rows.shape[-1]
    part_rows = narrow_count * row_count
    halo_list = halo_rows.reshape(-1)
    pick = (halo_list[:, None] == jnp.arange(row_count, dtype=jnp.int32)[None, :]).astype(
        jnp.bfloat16
    )
    halo_send = jnp.dot(pick, node_feats, preferred_element_type=jnp.float32).astype(jnp.bfloat16)
    halo_send = jnp.broadcast_to(
        halo_send.reshape(wide_count, 1, halo_peer, feat_width),
        (wide_count, narrow_count, halo_peer, feat_width),
    ).reshape(device_count, halo_peer, feat_width)
    received = lax.all_to_all(halo_send, ALL, split_axis=0, concat_axis=0, tiled=True)
    partition = lax.all_gather(node_feats, NARROW, axis=0, tiled=True)
    halo_id = edge_src - part_rows
    per_narrow = wide_count * halo_peer
    from_narrow = halo_id // per_narrow
    from_wide = (halo_id % per_narrow) // halo_peer
    arrival = part_rows + (from_wide * narrow_count + from_narrow) * halo_peer + halo_id % halo_peer
    edge_src = jnp.where(edge_src < part_rows, edge_src, arrival)

    dest_proj = jnp.dot(node_feats, dest_weight, preferred_element_type=jnp.float32)
    src_table = jnp.concatenate([partition, received.reshape(-1, feat_width)], axis=0)
    src_table = jnp.dot(src_table, source_weight, preferred_element_type=jnp.float32).astype(
        jnp.bfloat16
    )
    tile_count = row_count // TILE
    dest_gates = dest_proj[:, :feat_width].reshape(tile_count, TILE, feat_width)
    agg = lax.map(
        lambda tile_items: tile_sums(src_table, tile_items[0], tile_items[1], tile_items[2]),
        (edge_src, edge_dst, dest_gates),
    )
    agg = agg.reshape(row_count, feat_width)
    graph_out = graph_update(node_feats, dest_proj, agg, norm_gain)
    expert_count = router_weight.shape[1]
    logits = jnp.dot(graph_out, router_weight, preferred_element_type=jnp.float32)
    route_first = routes[:, 0]
    route_second = routes[:, 1]
    expert_range = jnp.arange(expert_count, dtype=jnp.int32)[None, :]
    hit_first = (route_first[:, None] == expert_range).astype(jnp.float32)
    hit_second = (route_second[:, None] == expert_range).astype(jnp.float32)
    hit_gap = hit_first - hit_second
    weight_first = jax.nn.sigmoid(jnp.sum(logits * hit_gap, axis=1))
    weight_second = 1.0 - weight_first
    combine = jnp.stack([weight_first, weight_second], axis=1)
    cot_float = cotangent.astype(jnp.float32)
    expert_grads = (combine[:, :, None] * cot_float[:, None, :]).astype(jnp.bfloat16)
    hits = jnp.concatenate([hit_first, hit_second], axis=0).astype(jnp.bfloat16)
    pair_ids = jnp.arange(2 * row_count, dtype=jnp.int32)
    earlier = (pair_ids[None, :] < pair_ids[:, None]).astype(jnp.bfloat16)
    ahead = jnp.dot(earlier, hits, preferred_element_type=jnp.float32)
    position = jnp.sum(ahead * hits.astype(jnp.float32), axis=1).astype(jnp.int32)
    capacity = 4 * row_count // expert_count
    slot_index = jnp.concatenate([route_first, route_second]) * capacity + position
    slot_range = jnp.arange(expert_count * capacity, dtype=jnp.int32)
    to_slot = (slot_range[:, None] == slot_index[None, :]).astype(jnp.bfloat16)
    send_rows = jnp.dot(
        to_slot, jnp.concatenate([graph_out, graph_out], axis=0), preferred_element_type=jnp.float32
    ).astype(jnp.bfloat16)
    send_grads = jnp.dot(
        to_slot,
        jnp.concatenate([expert_grads[:, 0], expert_grads[:, 1]], axis=0),
        preferred_element_type=jnp.float32,
    ).astype(jnp.bfloat16)
    send_shape = (expert_count, capacity, feat_width)

    def swap(rows):
        return lax.all_to_all(
            rows.reshape(send_shape), OWNERS, split_axis=0, concat_axis=0, tiled=True
        ).reshape(-1, feat_width)

    weight_in = lax.all_to_all(
        jnp.concatenate([expert_in, expert_in], axis=0), NARROW, split_axis=0, concat_axis=0, tiled=True
    )
    weight_out = lax.all_to_all(
        jnp.concatenate([expert_out, expert_out], axis=0), NARROW, split_axis=0, concat_axis=0, tiled=True
    )
    rows_in = swap(send_rows)
    grads_in = swap(send_grads)
    hidden = jnp.einsum("rd,mdh->mrh", rows_in, weight_in, preferred_element_type=jnp.float32)
    activated, gelu_back = jax.vjp(jax.nn.gelu, hidden)
    act_low = activated.astype(jnp.bfloat16)
    outputs = jnp.einsum(
        "mrh,mhd->rd", act_low, weight_out, preferred_element_type=jnp.float32
    ).astype(jnp.bfloat16)
    act_grad = jnp.einsum("rd,mhd->mrh", grads_in, weight_out, preferred_element_type=jnp.float32)
    hidden_grad = gelu_back(act_grad)[0].astype(jnp.bfloat16)
    grad_rows = jnp.einsum(
        "mrh,mdh->rd", hidden_grad, weight_in, preferred_element_type=jnp.float32
    ).astype(jnp.bfloat16)
    grad_w_in = jnp.einsum(
        "rd,mrh->mdh", rows_in, hidden_grad, preferred_element_type=jnp.float32
    ).astype(jnp.bfloat16)
    grad_w_out = jnp.einsum(
        "mrh,rd->mhd", act_low, grads_in, preferred_element_type=jnp.float32
    ).astype(jnp.bfloat16)

    def home(grads):
        back = lax.all_to_all(grads, NARROW, split_axis=0, concat_axis=0, tiled=True)
        return back[:2].astype(jnp.float32) + back[2:].astype(jnp.float32)

    back_out = swap(outputs)
    back_grad = swap(grad_rows)
    grad_expert_in = home(grad_w_in)
    grad_expert_out = home(grad_w_out)
    picked_y = lax.dot_general(
        to_slot, back_out, (((0,), (0,)), ((), ())), preferred_element_type=jnp.float32
    )
    picked_dx = lax.dot_general(
        to_slot, back_grad, (((0,), (0,)), ((), ())), preferred_element_type=jnp.float32
    )
    y_first, y_second = picked_y[:row_count], picked_y[row_count:]
    dx_first, dx_second = picked_dx[:row_count], picked_dx[row_count:]
    first_col, second_col = weight_first[:, None], weight_second[:, None]
    layer_out = (
        graph_out.astype(jnp.float32) + (first_col * y_first + second_col * y_second)
    ).astype(jnp.bfloat16)
    gap_grad = jnp.sum(cot_float * (y_first - y_second), axis=1) * weight_first * weight_second
    spread = jnp.dot(
        hit_gap.astype(jnp.bfloat16), router_weight.T, preferred_element_type=jnp.float32
    )
    grad_features = (
        cot_float + (first_col * dx_first + second_col * dx_second) + gap_grad[:, None] * spread
    )
    dlogits = gap_grad[:, None] * hit_gap
    high = dlogits.astype(jnp.bfloat16)
    low = (dlogits - high.astype(jnp.float32)).astype(jnp.bfloat16)
    halves = lax.dot_general(
        jnp.concatenate([high, low], axis=1),
        graph_out,
        (((0,), (0,)), ((), ())),
        preferred_element_type=jnp.float32,
    )
    partial_router = halves[:expert_count] + halves[expert_count:]
    pieces = lax.all_to_all(
        partial_router.reshape(device_count, -1, 128), ALL, split_axis=0, concat_axis=0, tiled=True
    )
    piece = jnp.sum(pieces, axis=0, keepdims=True)
    copies = jnp.broadcast_to(piece, (device_count,) + piece.shape[1:])
    whole = lax.all_to_all(copies, ALL, split_axis=0, concat_axis=0, tiled=True)
    grad_router = whole.reshape(expert_count, feat_width).T
    return (layer_out, grad_features, grad_expert_in, grad_expert_out, grad_router)


def solution(mesh):
    wide_count, narrow_count = mesh.devices.shape
    fine = Mesh(mesh.devices.reshape(wide_count, narrow_count // 2, 2), ALL)
    placed = (
        P(ALL, None),
        P("wide", NARROW, None, None),
        P(ALL, None),
        P(ALL, None),
        P(),
        P(),
        P(),
        P(),
        P(ALL, None),
        P("wide", None, NARROW),
        P("wide", NARROW, None),
        P(ALL, None),
    )
    return jax.shard_map(
        on_device,
        mesh=fine,
        in_specs=placed,
        out_specs=(
            P(ALL, None),
            P(ALL, None),
            P("wide", None, NARROW),
            P("wide", NARROW, None),
            P(),
        ),
        check_vma=False,
    )
```

```python
import functools

import jax
import jax.numpy as jnp
from jax import lax
from jax.experimental import pallas as pl
from jax.experimental.pallas import tpu as pltpu
from jax.sharding import Mesh
from jax.sharding import PartitionSpec as P

TILE = 128
CHUNK = 256
ALL = ("wide", "hi", "lo")
NARROW = ("hi", "lo")
OWNERS = ("wide", "lo")
F32 = jnp.float32
BF16 = jnp.bfloat16
I32 = jnp.int32
VMEM_LIMIT = 52 * 1024 * 1024


def mm(a, b, over=((1,), (0,))):
    return lax.dot_general(a, b, (over, ((), ())), preferred_element_type=F32)


def lanes(shape):
    return lax.broadcasted_iota(I32, shape, len(shape) - 1)


def sublanes(shape):
    return lax.broadcasted_iota(I32, shape, len(shape) - 2)


def one_hot(hit):
    return jnp.where(hit, 1.0, 0.0).astype(BF16)


def call(kernel, outs, args, scratch=(), smem=()):
    in_specs = [
        pl.BlockSpec(memory_space=pltpu.SMEM if i in smem else pltpu.VMEM) for i in range(len(args))
    ]
    return pl.pallas_call(
        kernel,
        out_shape=outs,
        in_specs=in_specs,
        out_specs=jax.tree.map(lambda _: pl.BlockSpec(memory_space=pltpu.VMEM), outs),
        scratch_shapes=list(scratch),
        compiler_params=pltpu.CompilerParams(vmem_limit_bytes=VMEM_LIMIT),
    )(*args)


def array(shape, dtype):
    return jax.ShapeDtypeStruct(shape, dtype)


def edge_kernel(
    keys,
    key_col,
    key_row,
    own,
    near,
    mid,
    far,
    halo,
    source_weight,
    dest_weight,
    norm_gain,
    router_weight,
    routes,
    slot_row,
    cotangent,
    graph_out,
    weight_first,
    send,
    table,
    dest_parts,
    self_part,
    picked,
    totals,
):
    rows, width = own.shape
    part_rows = 4 * rows
    for s, part in enumerate((own, near, mid, far)):
        table[s * rows : (s + 1) * rows] = mm(part[...], source_weight[...]).astype(BF16)

    def project(b, carry):
        at = pl.multiple_of(b * CHUNK, CHUNK)
        to = pl.multiple_of(part_rows + b * CHUNK, CHUNK)
        table[pl.ds(to, CHUNK), :] = mm(halo[pl.ds(at, CHUNK), :], source_weight[...]).astype(BF16)
        return carry

    lax.fori_loop(0, halo.shape[0] // CHUNK, project, 0)

    dest = mm(own[...], dest_weight[...])
    high = dest[:, :width].astype(BF16)
    low = (dest[:, :width] - high.astype(F32)).astype(BF16)
    tiles = rows // TILE
    for t in range(tiles):
        dest_parts[t, :TILE] = high[t * TILE : (t + 1) * TILE]
        dest_parts[t, TILE:] = low[t * TILE : (t + 1) * TILE]
    self_part[...] = dest[:, width:]
    totals[...] = jnp.zeros_like(totals)
    chunks = keys.shape[1] // CHUNK

    def one_chunk(step, carry):
        t = step // chunks
        c = step % chunks
        start = pl.multiple_of(c * CHUNK, CHUNK)
        first = keys[t, c * CHUNK] >> 16
        last = keys[t, c * CHUNK + CHUNK - 1] >> 16
        key = key_col[t, pl.ds(start, CHUNK), :]
        row = key >> 8
        dst = key & 255
        spot = lanes((CHUNK, CHUNK))

        def gather(b):
            at = pl.multiple_of(b * CHUNK, CHUNK)
            return mm(one_hot(row - b * CHUNK == spot), table[pl.ds(at, CHUNK), :])

        picked[...] = gather(first)

        def more(b, inner):
            picked[...] += gather(b)
            return inner

        lax.fori_loop(first + 1, last + 1, more, 0)
        dest_gate = mm(one_hot(dst == (spot & (TILE - 1))), dest_parts[t])
        gates = jax.nn.sigmoid(picked[:, :width] + dest_gate).astype(BF16)
        messages = (gates.astype(F32) * picked[:, width:]).astype(BF16)
        dst_row = key_row[t, :, pl.ds(start, CHUNK)] & 255
        selector = one_hot(dst_row == sublanes((TILE, CHUNK)))
        totals[t, :, :width] += mm(selector, messages)
        totals[t, :, width:] += mm(selector, gates)
        return carry

    lax.fori_loop(0, tiles * chunks, one_chunk, 0)

    whole = totals[...].reshape(rows, 2 * width)
    agg = whole[:, :width] / jnp.maximum(whole[:, width:], 1.0)
    pre_norm = self_part[...] + agg
    average = jnp.mean(pre_norm, axis=1, keepdims=True)
    center = pre_norm - average
    variance = jnp.mean(center * center, axis=1, keepdims=True)
    normed = center * lax.rsqrt(variance + 1e-05) * norm_gain[...]
    result = (own[...].astype(F32) + jnp.maximum(normed, 0.0)).astype(BF16)
    graph_out[...] = result

    logits = mm(result, router_weight[...])
    gap_mask = hit_gap(routes, logits.shape)
    first_weight = jax.nn.sigmoid(jnp.sum(logits * gap_mask, axis=1, keepdims=True))
    weight_first[...] = first_weight
    cot = cotangent[...].astype(F32)
    grads_first = (first_weight * cot).astype(BF16)
    grads_second = ((1.0 - first_weight) * cot).astype(BF16)
    experts, _, capacity, _ = send.shape
    slot = sublanes((experts * capacity, rows))
    to_first = one_hot(slot_row[0:1, :] == slot)
    to_second = one_hot(slot_row[1:2, :] == slot)
    rows_out = mm(to_first + to_second, result)
    send[:, 0] = rows_out.astype(BF16).reshape(experts, capacity, width)
    grads_out = mm(to_first, grads_first) + mm(to_second, grads_second)
    send[:, 1] = grads_out.astype(BF16).reshape(experts, capacity, width)


def hit_gap(routes, shape):
    spot = lanes(shape)
    first = jnp.where(routes[:, 0:1] == spot, 1.0, 0.0)
    second = jnp.where(routes[:, 1:2] == spot, 1.0, 0.0)
    return first - second


def gelu_parts(x):
    cubic = 0.7978845608028654 * (x + 0.044715 * (x * x * x))
    tanh = jnp.tanh(cubic)
    return tanh, 0.5 * x * (1.0 + tanh)


def forward_kernel(arrived, *refs):
    ins, outs, result = refs[:4], refs[4:8], refs[8]
    experts, _, capacity, width = arrived.shape
    step = CHUNK // capacity

    def block(b, carry):
        rows = arrived[pl.ds(b * step, step), 0].reshape(CHUNK, width)
        total = None
        for w_in, w_out in zip(ins, outs):
            active = gelu_parts(mm(rows, w_in[...]))[1].astype(BF16)
            part = mm(active, w_out[...])
            total = part if total is None else total + part
        result[pl.ds(pl.multiple_of(b * CHUNK, CHUNK), CHUNK), :] = total.astype(BF16)
        return carry

    lax.fori_loop(0, experts * capacity // CHUNK, block, 0)


def backward_kernel(arrived, *refs):
    ins, outs = refs[:4], refs[4:8]
    grad_rows = refs[8]
    grad_ins, grad_outs = refs[9:13], refs[13:17]
    act_all, hidden_all = refs[17], refs[18]
    experts, _, capacity, width = arrived.shape
    step = CHUNK // capacity

    def block(b, carry):
        at = pl.ds(pl.multiple_of(b * CHUNK, CHUNK), CHUNK)
        rows = arrived[pl.ds(b * step, step), 0].reshape(CHUNK, width)
        grads = arrived[pl.ds(b * step, step), 1].reshape(CHUNK, width)
        total = None
        for s, (w_in, w_out) in enumerate(zip(ins, outs)):
            x = mm(rows, w_in[...])
            tanh, active = gelu_parts(x)
            act_all[s, at, :] = active.astype(BF16)
            slope = 0.7978845608028654 * (1.0 + 0.134145 * (x * x))
            back = 0.5 * (1.0 + tanh) + 0.5 * x * (1.0 - tanh * tanh) * slope
            hidden = (back * mm(grads, w_out[...], ((1,), (1,)))).astype(BF16)
            hidden_all[s, at, :] = hidden
            part = mm(hidden, w_in[...], ((1,), (1,)))
            total = part if total is None else total + part
        grad_rows[at, :] = total.astype(BF16)
        return carry

    lax.fori_loop(0, experts * capacity // CHUNK, block, 0)
    rows = arrived[:, 0].reshape(experts * capacity, width)
    grads = arrived[:, 1].reshape(experts * capacity, width)
    for s in range(4):
        grad_ins[s][...] = mm(rows, hidden_all[s], ((0,), (0,))).astype(BF16)
        grad_outs[s][...] = mm(act_all[s], grads, ((0,), (0,))).astype(BF16)


def output_kernel(
    back, slot_col, graph_out, weight_first, cotangent, routes, layer_out, gap_grad, router_part
):
    rows = graph_out.shape[0]
    experts = router_part.shape[0]
    slot = lanes((rows, back.shape[0]))
    first = mm(one_hot(slot_col[:, 0:1] == slot), back[...])
    second = mm(one_hot(slot_col[:, 1:2] == slot), back[...])
    one, two = weight_first[...], 1.0 - weight_first[...]
    layer_out[...] = (graph_out[...].astype(F32) + (one * first + two * second)).astype(BF16)
    cot = cotangent[...].astype(F32)
    gap = jnp.sum(cot * (first - second), axis=1, keepdims=True) * one * two
    gap_grad[...] = gap
    dlogits = gap * hit_gap(routes, (rows, experts))
    high = dlogits.astype(BF16)
    low = (dlogits - high.astype(F32)).astype(BF16)
    over = ((0,), (0,))
    router_part[...] = mm(high, graph_out[...], over) + mm(low, graph_out[...], over)


def input_kernel(back, slot_col, gap_grad, weight_first, cotangent, routes, router_t, grad):
    rows = cotangent.shape[0]
    slot = lanes((rows, back.shape[0]))
    first = mm(one_hot(slot_col[:, 0:1] == slot), back[...])
    second = mm(one_hot(slot_col[:, 1:2] == slot), back[...])
    one, two = weight_first[...], 1.0 - weight_first[...]
    spread = mm(hit_gap(routes, (rows, router_t.shape[0])).astype(BF16), router_t[...])
    grad[...] = cotangent[...].astype(F32) + (one * first + two * second) + gap_grad[...] * spread


def halo_kernel(list_col, node_feats, send):
    rows, width = node_feats.shape
    pick = one_hot(list_col[...] == lanes((list_col.shape[0], rows)))
    chosen = mm(pick, node_feats[...]).astype(BF16)
    wide, narrow, peer, _ = send.shape
    for n in range(narrow):
        send[:, n] = chosen.reshape(wide, peer, width)


def ring(n, s):
    return [(i, (i + s) % n) for i in range(n)]


def total_over_all(value, wide_count):
    def moved(v, names, pairs):
        return lax.ppermute(v, names, pairs).astype(F32)

    def along(unit, shift):
        def to(i):
            return i - (i // unit % 4) * unit + ((i // unit + shift) % 4) * unit

        return [(i, to(i)) for i in range(wide_count)]

    value = value.astype(BF16)
    value = value.astype(F32) + moved(value, "wide", [(i, i ^ 1) for i in range(wide_count)])
    axes = [("wide", lambda s: along(2, s)), ("wide", lambda s: along(8, s))]
    axes.append((NARROW, lambda s: ring(4, s)))
    for names, pairs in axes:
        sent = value.astype(BF16)
        one, two, three = (moved(sent, names, pairs(s)) for s in (1, 2, 3))
        value = (sent.astype(F32) + two) + (one + three)
    return value


def on_device(
    node_feats,
    halo_rows,
    edge_src,
    edge_dst,
    dest_weight,
    source_weight,
    norm_gain,
    router_weight,
    routes,
    expert_in,
    expert_out,
    cotangent,
):
    rows, width = node_feats.shape
    wide_count = lax.axis_size("wide")
    narrow_count = lax.axis_size("hi") * lax.axis_size("lo")
    device_count = wide_count * narrow_count
    my_lo = lax.axis_index("lo")
    me = lax.axis_index("hi") * 2 + my_lo
    peer = halo_rows.shape[-1]
    part_rows = narrow_count * rows
    experts = router_weight.shape[1]
    capacity = 4 * rows // experts
    tiles, slots = edge_src.shape

    halo_send = call(
        halo_kernel,
        array((wide_count, narrow_count, peer, width), BF16),
        (halo_rows.reshape(-1, 1), node_feats),
    )
    received = lax.all_to_all(
        halo_send.reshape(device_count, peer, width), ALL, split_axis=0, concat_axis=0, tiled=True
    )
    parts = [node_feats] + [
        lax.ppermute(node_feats, NARROW, ring(narrow_count, s)) for s in range(1, narrow_count)
    ]

    own_id = (me - edge_src // rows) % narrow_count * rows + edge_src % rows
    halo_id = edge_src - part_rows
    per_narrow = wide_count * peer
    from_narrow = halo_id // per_narrow
    from_wide = (halo_id % per_narrow) // peer
    halo_id = part_rows + (from_wide * narrow_count + from_narrow) * peer + halo_id % peer
    place = jnp.where(edge_src < part_rows, own_id, halo_id)
    keys = lax.sort(place * 256 + edge_dst, dimension=1)

    route_rows = routes.T.reshape(-1)
    hits = (route_rows[:, None] == jnp.arange(experts, dtype=I32)[None, :]).astype(BF16)
    pair_ids = jnp.arange(2 * rows, dtype=I32)
    earlier = (pair_ids[None, :] < pair_ids[:, None]).astype(BF16)
    ahead = jnp.dot(earlier, hits, preferred_element_type=F32)
    position = jnp.sum(ahead * hits.astype(F32), axis=1).astype(I32)
    slot_row = (route_rows * capacity + position).reshape(2, rows)
    slot_col = slot_row.T

    graph_out, weight_first, send = call(
        edge_kernel,
        (
            array((rows, width), BF16),
            array((rows, 1), F32),
            array((experts, 2, capacity, width), BF16),
        ),
        (
            keys,
            keys.reshape(tiles, slots, 1),
            keys.reshape(tiles, 1, slots),
            *parts,
            received.reshape(-1, width),
            source_weight,
            dest_weight,
            norm_gain.reshape(1, width),
            router_weight,
            routes,
            slot_row,
            cotangent,
        ),
        scratch=(
            pltpu.VMEM((part_rows + device_count * peer, 2 * width), BF16),
            pltpu.VMEM((tiles, 2 * TILE, width), BF16),
            pltpu.VMEM((rows, width), F32),
            pltpu.VMEM((CHUNK, 2 * width), F32),
            pltpu.VMEM((tiles, TILE, 2 * width), F32),
        ),
        smem=(0,),
    )
    arrived = lax.all_to_all(
        send.reshape(experts, 2 * capacity, width), OWNERS, split_axis=0, concat_axis=0, tiled=True
    ).reshape(experts, 2, capacity, width)

    weights = [expert_in, expert_out]
    received, weights = lax.optimization_barrier((received, weights))
    blocks = []
    for weight in weights:
        mine = lax.dynamic_index_in_dim(weight, my_lo, 0, keepdims=False)
        other = lax.dynamic_index_in_dim(weight, 1 - my_lo, 0, keepdims=False)
        blocks.append(mine)
        for s in range(1, narrow_count):
            sent = other if s % 2 else mine
            blocks.append(lax.ppermute(sent, NARROW, ring(narrow_count, s)))
    flat = array((experts * capacity, width), BF16)
    outputs = call(forward_kernel, flat, (arrived, *blocks))
    hidden_block = expert_in.shape[2]
    grad_shapes = [array((width, hidden_block), BF16)] * 4 + [array((hidden_block, width), BF16)] * 4
    saved = pltpu.VMEM((4, experts * capacity, hidden_block), BF16)
    grad_rows, *grad_blocks = call(
        backward_kernel, (flat, *grad_shapes), (arrived, *blocks), scratch=(saved, saved)
    )

    def swap(values):
        return lax.all_to_all(
            values.reshape(experts, capacity, width), OWNERS, split_axis=0, concat_axis=0, tiled=True
        ).reshape(-1, width)

    def home(grads):
        back = [grads[0]] + [
            lax.ppermute(grads[s], NARROW, ring(narrow_count, -s)) for s in range(1, narrow_count)
        ]
        mine = back[0].astype(F32) + back[2].astype(F32)
        other = back[1].astype(F32) + back[3].astype(F32)
        low = my_lo == 0
        return jnp.stack([jnp.where(low, mine, other), jnp.where(low, other, mine)])

    back_out = swap(outputs)
    grad_expert_in = home(grad_blocks[:4])
    grad_expert_out = home(grad_blocks[4:])
    layer_out, gap_grad, router_part = call(
        output_kernel,
        (array((rows, width), BF16), array((rows, 1), F32), array((experts, width), F32)),
        (back_out, slot_col, graph_out, weight_first, cotangent, routes),
    )
    back_grad = swap(grad_rows)
    grad_features = call(
        input_kernel,
        array((rows, width), F32),
        (back_grad, slot_col, gap_grad, weight_first, cotangent, routes, router_weight.T),
    )
    grad_router = total_over_all(router_part, wide_count).T
    return (layer_out, grad_features, grad_expert_in, grad_expert_out, grad_router)


def solution(mesh):
    wide_count, narrow_count = mesh.devices.shape
    fine = Mesh(mesh.devices.reshape(wide_count, narrow_count // 2, 2), ALL)
    placed = (
        P(ALL, None),
        P("wide", NARROW, None, None),
        P(ALL, None),
        P(ALL, None),
        P(),
        P(),
        P(),
        P(),
        P(ALL, None),
        P("wide", None, NARROW),
        P("wide", NARROW, None),
        P(ALL, None),
    )
    return jax.shard_map(
        on_device,
        mesh=fine,
        in_specs=placed,
        out_specs=(
            P(ALL, None),
            P(ALL, None),
            P("wide", None, NARROW),
            P("wide", NARROW, None),
            P(),
        ),
        check_vma=False,
    )
```

```python
import jax
import jax.numpy as jnp
from jax import lax
from jax.experimental import pallas as pl
from jax.experimental.pallas import tpu as pltpu
from jax.sharding import Mesh
from jax.sharding import PartitionSpec as P

TILE = 128
CHUNK = 256
WINDOW = 512
PANELS = 9
ALL = ("wide", "hi", "lo")
NARROW = ("hi", "lo")
OWNERS = ("wide", "lo")
F32 = jnp.float32
BF16 = jnp.bfloat16
I32 = jnp.int32
EARLY_IN = (1, 3)
SOON_IN = (2,)
SOON_OUT = (1, 3)
FLOPS_PER_US = 10**9
BYTES_PER_US = 3 * 10**6
VMEM_LIMIT = 52 * 1024 * 1024


def mm(a, b, over=((1,), (0,))):
    return lax.dot_general(a, b, (over, ((), ())), preferred_element_type=F32)


def lanes(shape):
    return lax.broadcasted_iota(I32, shape, len(shape) - 1)


def sublanes(shape):
    return lax.broadcasted_iota(I32, shape, len(shape) - 2)


def one_hot(hit):
    return jnp.where(hit, 1.0, 0.0).astype(BF16)


def call(kernel, outs, args, scratch=(), smem=(), cost=1):
    in_specs = [
        pl.BlockSpec(memory_space=pltpu.SMEM if i in smem else pltpu.VMEM) for i in range(len(args))
    ]
    return pl.pallas_call(
        kernel,
        out_shape=outs,
        in_specs=in_specs,
        out_specs=jax.tree.map(lambda _: pl.BlockSpec(memory_space=pltpu.VMEM), outs),
        scratch_shapes=list(scratch),
        compiler_params=pltpu.CompilerParams(vmem_limit_bytes=VMEM_LIMIT),
        cost_estimate=pl.CostEstimate(
            flops=cost * FLOPS_PER_US, transcendentals=0, bytes_accessed=cost * BYTES_PER_US
        ),
    )(*args)


def array(shape, dtype):
    return jax.ShapeDtypeStruct(shape, dtype)


def project(table, parts, weight):
    at = 0
    for part in parts:
        for start in range(0, part.shape[0], CHUNK):
            rows = mm(part[start : start + CHUNK], weight[...])
            table[at : at + CHUNK] = rows.astype(BF16)
            at += CHUNK
    table[at:] = jnp.zeros((WINDOW, table.shape[1]), BF16)


def split_dest(dest, dest_parts):
    high = dest.astype(BF16)
    low = (dest - high.astype(F32)).astype(BF16)
    for t in range(dest_parts.shape[0]):
        dest_parts[t, :TILE] = high[t * TILE : (t + 1) * TILE]
        dest_parts[t, TILE:] = low[t * TILE : (t + 1) * TILE]


def add_edges(t, chunks, base, limit, keys, key_col, key_row, table, dest_parts, picked, totals):
    width = dest_parts.shape[2]
    spot = lanes((CHUNK, WINDOW))
    tile_spot = lanes((CHUNK, 2 * TILE)) & (TILE - 1)

    def one_chunk(c, carry):
        start = pl.multiple_of(c * CHUNK, CHUNK)
        first = jnp.maximum((keys[t, c * CHUNK] >> 8) - base, 0) & ~15
        last = jnp.minimum(keys[t, c * CHUNK + CHUNK - 1] >> 8, limit - 1) - base
        key = key_col[t, pl.ds(start, CHUNK), :]
        row = (key >> 8) - (base + first)

        def gather(k):
            at = pl.multiple_of(first + k * WINDOW, 16)
            return mm(one_hot(row - k * WINDOW == spot), table[pl.ds(at, WINDOW), :])

        picked[...] = gather(0)

        def more(k, inner):
            picked[...] += gather(k)
            return inner

        lax.fori_loop(1, (last - first) // WINDOW + 1, more, 0)
        dest_gate = mm(one_hot((key & 255) == tile_spot), dest_parts[t])
        pre = picked[:, :width] + dest_gate
        gates = (0.5 * jnp.tanh(0.5 * pre) + 0.5).astype(BF16)
        messages = gates * picked[:, width:].astype(BF16)
        row_key = key_row[t, :, pl.ds(start, CHUNK)]
        source = row_key >> 8
        target = jnp.where((source >= base) & (source < limit), row_key & 255, 255)
        selector = one_hot(target == sublanes((TILE, CHUNK)))
        totals[t, :, :width] += mm(selector, messages)
        totals[t, :, width:] += mm(selector, gates)
        return carry

    lax.fori_loop(chunks[0], chunks[1], one_chunk, 0)


def near_kernel(
    keys,
    near_count,
    key_col,
    key_row,
    own,
    back_one,
    back_two,
    back_three,
    halo,
    source_weight,
    dest_weight,
    totals,
    dest,
    table,
    dest_parts,
    picked,
):
    rows, width = own.shape
    project(table, (own, back_one, back_two, back_three, halo), source_weight)
    dest[...] = mm(own[...], dest_weight[...])
    split_dest(dest[:, :width], dest_parts)
    totals[...] = jnp.zeros_like(totals)
    limit = 4 * rows + halo.shape[0]
    for t in range(rows // TILE):
        chunks = (0, (near_count[t] + CHUNK - 1) // CHUNK)
        add_edges(
            t, chunks, 0, limit, keys, key_col, key_row, table, dest_parts, picked, totals
        )


def far_kernel(
    keys,
    near_count,
    key_col,
    key_row,
    halo_one,
    halo_two,
    halo_three,
    source_weight,
    near_totals,
    dest,
    own,
    norm_gain,
    router_weight,
    routes,
    slot_row,
    cotangent,
    graph_out,
    weight_first,
    send,
    table,
    dest_parts,
    picked,
    totals,
):
    rows, width = own.shape
    project(table, (halo_one, halo_two, halo_three), source_weight)
    split_dest(dest[:, :width], dest_parts)
    totals[...] = near_totals[...]
    base = 4 * rows + halo_one.shape[0]
    limit = base + 3 * halo_one.shape[0]
    for t in range(rows // TILE):
        chunks = (near_count[t] // CHUNK, keys.shape[1] // CHUNK)
        add_edges(
            t, chunks, base, limit, keys, key_col, key_row, table, dest_parts, picked, totals
        )

    whole = totals[...].reshape(rows, 2 * width)
    agg = whole[:, :width] / jnp.maximum(whole[:, width:], 1.0)
    pre_norm = dest[:, width:] + agg
    average = jnp.mean(pre_norm, axis=1, keepdims=True)
    center = pre_norm - average
    variance = jnp.mean(center * center, axis=1, keepdims=True)
    normed = center * lax.rsqrt(variance + 1e-05) * norm_gain[...]
    result = (own[...].astype(F32) + jnp.maximum(normed, 0.0)).astype(BF16)
    graph_out[...] = result

    logits = mm(result, router_weight[...])
    gap_mask = hit_gap(routes, logits.shape)
    first_weight = jax.nn.sigmoid(jnp.sum(logits * gap_mask, axis=1, keepdims=True))
    weight_first[...] = first_weight
    cot = cotangent[...].astype(F32)
    grads_first = (first_weight * cot).astype(BF16)
    grads_second = ((1.0 - first_weight) * cot).astype(BF16)
    experts = router_weight.shape[1]
    capacity = send.shape[1] // PANELS
    slot = sublanes((experts * capacity, rows))
    to_first = one_hot(slot_row[0:1, :] == slot)
    to_second = one_hot(slot_row[1:2, :] == slot)
    rows_out = mm(to_first + to_second, result).astype(BF16)
    grads_out = (mm(to_first, grads_first) + mm(to_second, grads_second)).astype(BF16)
    about_first = about(1.0 - first_weight, routes[:, 1:2])
    about_second = about(first_weight, routes[:, 0:1])
    about_out = (mm(to_first, about_first) + mm(to_second, about_second)).astype(BF16)
    panels = [v[:, i : i + 128] for v in (rows_out, grads_out) for i in range(0, width, 128)]
    for p, panel in enumerate(panels + [about_out]):
        send[:, p * capacity : (p + 1) * capacity] = panel.reshape(experts, capacity, 128)


def about(weight, expert):
    high = weight.astype(BF16).astype(F32)
    lane = lanes((weight.shape[0], 128))
    parts = jnp.where(lane == 0, high, jnp.where(lane == 1, weight - high, 0.0))
    return jnp.where(lane == 2, expert.astype(F32), parts).astype(BF16)


def hit_gap(routes, shape):
    spot = lanes(shape)
    first = jnp.where(routes[:, 0:1] == spot, 1.0, 0.0)
    second = jnp.where(routes[:, 1:2] == spot, 1.0, 0.0)
    return first - second


def unpack(arrived, chunks, capacity, start, count):
    parts = [
        arrived[chunks, p * capacity : (p + 1) * capacity].reshape(-1, 128)
        for p in range(start, start + count)
    ]
    return jnp.concatenate(parts, axis=1)


def expert_kernel(expert, arrived, *refs):
    ins, outs = refs[:4], refs[4:8]
    back, router_part, act_all, hidden_all, router_sum = refs[8:]
    chunk_count = arrived.shape[0]
    _, _, capacity, width = back.shape
    step = CHUNK // capacity
    experts = router_part.shape[0]
    router_sum[...] = jnp.zeros_like(router_sum)

    def block(b, carry):
        at = pl.ds(pl.multiple_of(b * CHUNK, CHUNK), CHUNK)
        chunks = pl.ds(b * step, step)
        rows = unpack(arrived, chunks, capacity, 0, 4)
        grads = unpack(arrived, chunks, capacity, 4, 4)
        other = unpack(arrived, chunks, capacity, 8, 1).astype(F32)
        y, dx = None, None
        for s, (w_in, w_out) in enumerate(zip(ins, outs)):
            x = mm(rows, w_in[...])
            square = x * x
            tanh = jnp.tanh(x * (0.7978845608028654 + 0.035677408136300125 * square))
            half = 0.5 + 0.5 * tanh
            active = (x * half).astype(BF16)
            slope = 0.7978845608028654 + 0.10703222440890037 * square
            back_slope = half + 0.5 * x * (1.0 - tanh * tanh) * slope
            hidden = (back_slope * mm(grads, w_out[...], ((1,), (1,)))).astype(BF16)
            act_all[s, at, :] = active
            hidden_all[s, at, :] = hidden
            y_part = mm(active, w_out[...])
            dx_part = mm(hidden, w_in[...], ((1,), (1,)))
            y = y_part if y is None else y + y_part
            dx = dx_part if dx is None else dx + dx_part
        back[chunks, 0] = y.astype(BF16).reshape(step, capacity, width)
        back[chunks, 1] = dx.astype(BF16).reshape(step, capacity, width)
        share = jnp.sum(grads.astype(F32) * y, axis=1, keepdims=True)
        share = share * (other[:, 0:1] + other[:, 1:2])
        lane = lanes((CHUNK, experts))
        own_lane = jnp.where(lane == expert[0], 1.0, 0.0)
        other_lane = jnp.where(lane.astype(F32) == other[:, 2:3], 1.0, 0.0)
        shares = share * (own_lane - other_lane)
        high = shares.astype(BF16)
        low = (shares - high.astype(F32)).astype(BF16)
        router_sum[...] += mm(high, rows, ((0,), (0,))) + mm(low, rows, ((0,), (0,)))
        return carry

    lax.fori_loop(0, chunk_count // step, block, 0)
    router_part[...] = router_sum[...]


def weight_kernel(arrived, act_all, hidden_all, *blocks):
    capacity = arrived.shape[1] // PANELS
    rows = unpack(arrived, slice(None), capacity, 0, 4)
    grads = unpack(arrived, slice(None), capacity, 4, 4)
    for s in range(4):
        blocks[s][...] = mm(rows, hidden_all[s], ((0,), (0,))).astype(BF16)
        blocks[4 + s][...] = mm(act_all[s], grads, ((0,), (0,))).astype(BF16)


def output_kernel(
    back,
    slot_col,
    graph_out,
    weight_first,
    cotangent,
    routes,
    router_t,
    layer_out,
    grad_features,
):
    rows, width = graph_out.shape
    slot = lanes((rows, slot_col.shape[1] // 2 * back.shape[0] * back.shape[2]))
    to_first = one_hot(slot_col[:, 0:1] == slot)
    to_second = one_hot(slot_col[:, 1:2] == slot)
    one, two = weight_first[...], 1.0 - weight_first[...]
    y = back[:, 0].reshape(-1, width)
    first, second = mm(to_first, y), mm(to_second, y)
    layer_out[...] = (graph_out[...].astype(F32) + (one * first + two * second)).astype(BF16)
    cot = cotangent[...].astype(F32)
    gap = jnp.sum(cot * (first - second), axis=1, keepdims=True) * one * two
    dx = back[:, 1].reshape(-1, width)
    mixed = one * mm(to_first, dx) + two * mm(to_second, dx)
    spread = mm(hit_gap(routes, (rows, router_t.shape[0])).astype(BF16), router_t[...])
    grad_features[...] = cot + mixed + gap * spread


def halo_kernel(list_col, node_feats, send):
    pick = one_hot(list_col[...] == lanes((list_col.shape[0], node_feats.shape[0])))
    send[...] = mm(pick, node_feats[...]).astype(BF16).reshape(send.shape)


def hold(values):
    return lax.optimization_barrier(values)


def ring(n, s):
    return [(i, (i + s) % n) for i in range(n)]


def along(wide_count, unit, shift):
    def to(i):
        return i - (i // unit % 4) * unit + ((i // unit + shift) % 4) * unit

    return [(i, to(i)) for i in range(wide_count)]


def add_axis(value, names, pairs):
    sent = value.astype(BF16)
    one, two, three = (lax.ppermute(sent, names, pairs(s)).astype(F32) for s in (1, 2, 3))
    return (sent.astype(F32) + two) + (one + three)


def on_device(
    node_feats,
    halo_rows,
    edge_src,
    edge_dst,
    dest_weight,
    source_weight,
    norm_gain,
    router_weight,
    routes,
    expert_in,
    expert_out,
    cotangent,
):
    rows, width = node_feats.shape
    wide_count = lax.axis_size("wide")
    narrow_count = lax.axis_size("hi") * lax.axis_size("lo")
    my_lo = lax.axis_index("lo")
    me = lax.axis_index("hi") * 2 + my_lo
    peer = halo_rows.shape[-1]
    part_rows = narrow_count * rows
    experts = router_weight.shape[1]
    capacity = 4 * rows // experts
    tiles, slots = edge_src.shape

    def around(value, s):
        return lax.ppermute(value, NARROW, ring(narrow_count, s))

    def weight_to(weight, s):
        which = (my_lo + s) % 2
        return lax.dynamic_index_in_dim(weight, which, 0, keepdims=False)

    in_blocks = [weight_to(expert_in, 0)] + [None] * 3
    out_blocks = [weight_to(expert_out, 0)] + [None] * 3

    per_narrow = wide_count * peer
    local = edge_src < part_rows
    halo_id = edge_src - part_rows
    size = jnp.where(local, rows, per_narrow)
    offset = jnp.where(local, edge_src, halo_id)
    place = (me - offset // size) % narrow_count * size + offset % size
    place = place + jnp.where(local, 0, part_rows)
    keys = lax.sort(place * 256 + edge_dst, dimension=1)
    near_rows = part_rows + per_narrow
    near_count = jnp.sum((keys < near_rows * 256).astype(I32), axis=1)
    key_col = keys.reshape(tiles, slots, 1)
    key_row = keys.reshape(tiles, 1, slots)

    halo_send = call(
        halo_kernel,
        array((wide_count, peer, width), BF16),
        (halo_rows.reshape(-1, 1), node_feats),
    )
    received = lax.all_to_all(halo_send, "wide", split_axis=0, concat_axis=0, tiled=True)
    received = received.reshape(-1, width)
    parts = [node_feats] + [around(node_feats, s) for s in range(1, narrow_count)]
    for s in EARLY_IN:
        in_blocks[s] = around(weight_to(expert_in, s), s)
    received, parts, in_blocks, keys, key_col, key_row, near_count = hold(
        (received, parts, in_blocks, keys, key_col, key_row, near_count)
    )
    halos = [received] + [around(received, s) for s in range(1, narrow_count)]

    route_rows = routes.T.reshape(-1)
    hits = (route_rows[:, None] == jnp.arange(experts, dtype=I32)[None, :]).astype(BF16)
    pair_ids = jnp.arange(2 * rows, dtype=I32)
    earlier = (pair_ids[None, :] < pair_ids[:, None]).astype(BF16)
    ahead = jnp.dot(earlier, hits, preferred_element_type=F32)
    position = jnp.sum(ahead * hits.astype(F32), axis=1).astype(I32)
    slot_row = (route_rows * capacity + position).reshape(2, rows)
    slot_col = slot_row.T

    near_totals, dest = call(
        near_kernel,
        (array((tiles, TILE, 2 * width), F32), array((rows, 2 * width), F32)),
        (keys, near_count, key_col, key_row, *parts, halos[0], source_weight, dest_weight),
        scratch=(
            pltpu.VMEM((near_rows + WINDOW, 2 * width), BF16),
            pltpu.VMEM((tiles, 2 * TILE, width), BF16),
            pltpu.VMEM((CHUNK, 2 * width), F32),
        ),
        smem=(0, 1),
        cost=14,
    )
    halos, near_totals, expert_in, expert_out = hold((halos, near_totals, expert_in, expert_out))
    for s in range(1, narrow_count):
        if s not in EARLY_IN:
            in_blocks[s] = around(weight_to(expert_in, s), s)
        out_blocks[s] = around(weight_to(expert_out, s), s)
    graph_out, weight_first, send = call(
        far_kernel,
        (
            array((rows, width), BF16),
            array((rows, 1), F32),
            array((experts, PANELS * capacity, 128), BF16),
        ),
        (
            keys,
            near_count,
            key_col,
            key_row,
            *halos[1:],
            source_weight,
            near_totals,
            dest,
            node_feats,
            norm_gain.reshape(1, width),
            router_weight,
            routes,
            slot_row,
            cotangent,
        ),
        scratch=(
            pltpu.VMEM((3 * per_narrow + WINDOW, 2 * width), BF16),
            pltpu.VMEM((tiles, 2 * TILE, width), BF16),
            pltpu.VMEM((CHUNK, 2 * width), F32),
            pltpu.VMEM((tiles, TILE, 2 * width), F32),
        ),
        smem=(0, 1),
        cost=18,
    )
    sooner = [in_blocks[s] for s in SOON_IN] + [out_blocks[s] for s in SOON_OUT]
    send, sooner = hold((send, sooner))
    for s, block in zip(SOON_IN, sooner):
        in_blocks[s] = block
    for s, block in zip(SOON_OUT, sooner[len(SOON_IN) :]):
        out_blocks[s] = block
    arrived = lax.all_to_all(send, OWNERS, split_axis=0, concat_axis=0, tiled=True)
    blocks = in_blocks + out_blocks
    hidden_block = expert_in.shape[2]
    expert = (lax.axis_index("wide") * 2 + my_lo).astype(I32).reshape(1)
    saved = array((4, experts * capacity, hidden_block), BF16)
    back, router_part, act_all, hidden_all = call(
        expert_kernel,
        (
            array((experts, 2, capacity, width), BF16),
            array((experts, width), F32),
            saved,
            saved,
        ),
        (expert, arrived, *blocks),
        scratch=(pltpu.VMEM((experts, width), F32),),
        smem=(0,),
        cost=12,
    )
    router_part = router_part.astype(BF16)
    twin = lax.ppermute(router_part, "wide", [(i, i ^ 1) for i in range(wide_count)])
    router_sum = router_part.astype(F32) + twin.astype(F32)
    back = lax.all_to_all(
        back.reshape(experts, 2 * capacity, width), OWNERS, split_axis=0, concat_axis=0, tiled=True
    ).reshape(experts, 2, capacity, width)
    grad_shapes = [array((width, hidden_block), BF16)] * 4 + [array((hidden_block, width), BF16)] * 4
    grad_blocks = call(weight_kernel, grad_shapes, (arrived, act_all, hidden_all), cost=5)

    def sent_home(grads):
        return [grads[0]] + [around(grads[s], -s) for s in range(1, narrow_count)]

    def home(back):
        mine = back[0].astype(F32) + back[2].astype(F32)
        other = back[1].astype(F32) + back[3].astype(F32)
        low = my_lo == 0
        return jnp.stack([jnp.where(low, mine, other), jnp.where(low, other, mine)])

    in_back = sent_home(grad_blocks[:4])
    out_back = sent_home(grad_blocks[4:])
    router_sum = add_axis(router_sum, NARROW, lambda s: ring(narrow_count, s))
    router_sum, back, in_back = hold((router_sum, back, in_back))
    router_sum = add_axis(router_sum, "wide", lambda s: along(wide_count, 2, s))
    router_sum, out_back = hold((router_sum, out_back))
    router_total = add_axis(router_sum, "wide", lambda s: along(wide_count, 8, s))
    layer_out, grad_features = call(
        output_kernel,
        (array((rows, width), BF16), array((rows, width), F32)),
        (back, slot_col, graph_out, weight_first, cotangent, routes, router_weight.T),
        cost=5,
    )
    grad_expert_in = home(in_back)
    grad_expert_out = home(out_back)
    grad_router = router_total.T
    return (layer_out, grad_features, grad_expert_in, grad_expert_out, grad_router)


def solution(mesh):
    wide_count, narrow_count = mesh.devices.shape
    fine = Mesh(mesh.devices.reshape(wide_count, narrow_count // 2, 2), ALL)
    placed = (
        P(ALL, None),
        P("wide", NARROW, None, None),
        P(ALL, None),
        P(ALL, None),
        P(),
        P(),
        P(),
        P(),
        P(ALL, None),
        P("wide", None, NARROW),
        P("wide", NARROW, None),
        P(ALL, None),
    )
    return jax.shard_map(
        on_device,
        mesh=fine,
        in_specs=placed,
        out_specs=(
            P(ALL, None),
            P(ALL, None),
            P("wide", None, NARROW),
            P("wide", NARROW, None),
            P(),
        ),
        check_vma=False,
    )
```

```python
import jax
import jax.numpy as jnp
from jax import lax
from jax.experimental import pallas as pl
from jax.experimental.pallas import tpu as pltpu
from jax.sharding import Mesh
from jax.sharding import PartitionSpec as P

TILE = 128
CHUNK = 256
WINDOW = 512
PANELS = 9
ALL = ("wide", "hi", "lo")
NARROW = ("hi", "lo")
OWNERS = ("wide", "lo")
F32 = jnp.float32
BF16 = jnp.bfloat16
I32 = jnp.int32
EARLY_IN = (1, 3)
SOON_IN = (2,)
SOON_OUT = (1, 3)
FLOPS_PER_US = 10**9
BYTES_PER_US = 3 * 10**6
VMEM_LIMIT = 52 * 1024 * 1024


def mm(a, b, over=((1,), (0,))):
    return lax.dot_general(a, b, (over, ((), ())), preferred_element_type=F32)


def lanes(shape):
    return lax.broadcasted_iota(I32, shape, len(shape) - 1)


def sublanes(shape):
    return lax.broadcasted_iota(I32, shape, len(shape) - 2)


def one_hot(hit):
    return jnp.where(hit, 1.0, 0.0).astype(BF16)


def call(kernel, outs, args, scratch=(), smem=(), cost=1):
    in_specs = [
        pl.BlockSpec(memory_space=pltpu.SMEM if i in smem else pltpu.VMEM) for i in range(len(args))
    ]
    return pl.pallas_call(
        kernel,
        out_shape=outs,
        in_specs=in_specs,
        out_specs=jax.tree.map(lambda _: pl.BlockSpec(memory_space=pltpu.VMEM), outs),
        scratch_shapes=list(scratch),
        compiler_params=pltpu.CompilerParams(vmem_limit_bytes=VMEM_LIMIT),
        cost_estimate=pl.CostEstimate(
            flops=cost * FLOPS_PER_US, transcendentals=0, bytes_accessed=cost * BYTES_PER_US
        ),
    )(*args)


def array(shape, dtype):
    return jax.ShapeDtypeStruct(shape, dtype)


def project(table, parts, weight):
    at = 0
    for part in parts:
        for start in range(0, part.shape[0], CHUNK):
            rows = mm(part[start : start + CHUNK], weight[...])
            table[at : at + CHUNK] = rows.astype(BF16)
            at += CHUNK
    table[at:] = jnp.zeros((WINDOW, table.shape[1]), BF16)


def split_dest(dest, dest_parts):
    high = dest.astype(BF16)
    low = (dest - high.astype(F32)).astype(BF16)
    for t in range(dest_parts.shape[0]):
        dest_parts[t, :TILE] = high[t * TILE : (t + 1) * TILE]
        dest_parts[t, TILE:] = low[t * TILE : (t + 1) * TILE]


def add_edges(chunks, base, limit, keys, key_col, key_row, table, dest_parts, picked, totals):
    width = dest_parts.shape[2]
    spot = lanes((CHUNK, WINDOW))
    tile_spot = lanes((CHUNK, 2 * TILE)) & (TILE - 1)

    def gather(t, c, k):
        first = jnp.clip((keys[t, c * CHUNK] >> 8) - base, 0, limit - base) & ~15
        at = pl.multiple_of(first + k * WINDOW, 16)
        key = key_col[t, pl.ds(pl.multiple_of(c * CHUNK, CHUNK), CHUNK), :]
        row = (key >> 8) - (base + at)
        return mm(one_hot(row == spot), table[pl.ds(at, WINDOW), :])

    def more(t, c):
        first = jnp.clip((keys[t, c * CHUNK] >> 8) - base, 0, limit - base) & ~15
        last = jnp.minimum(keys[t, c * CHUNK + CHUNK - 1] >> 8, limit - 1) - base

        def window(k, carry):
            picked[t][...] += gather(t, c, k)
            return carry

        lax.fori_loop(1, (jnp.maximum(last - first, 0) >> 9) + 1, window, 0)

    def add(t, c, live):
        start = pl.multiple_of(c * CHUNK, CHUNK)
        key = key_col[t, pl.ds(start, CHUNK), :]
        dest_gate = mm(one_hot((key & 255) == tile_spot), dest_parts[t])
        pre = picked[t][:, :width] + dest_gate
        gates = (0.5 * jnp.tanh(0.5 * pre) + 0.5).astype(BF16)
        messages = gates * picked[t][:, width:].astype(BF16)
        row_key = key_row[t, :, pl.ds(start, CHUNK)]
        source = row_key >> 8
        target = jnp.where((source >= base) & (source < limit) & live, row_key & 255, 255)
        selector = one_hot(target == sublanes((TILE, CHUNK)))
        totals[t, :, :width] += mm(selector, messages)
        totals[t, :, width:] += mm(selector, gates)

    picked[1][...] = jnp.zeros_like(picked[1])
    begin, end = chunks

    def both(c, carry):
        picked[0][...] = gather(0, c, 0)
        add(1, jnp.maximum(c - 1, 0), c > begin)
        more(0, c)
        picked[1][...] = gather(1, c, 0)
        add(0, c, c >= begin)
        more(1, c)
        return carry

    lax.fori_loop(begin, end, both, 0)
    add(1, jnp.maximum(end - 1, 0), end > begin)


def near_kernel(
    keys,
    near_count,
    key_col,
    key_row,
    own,
    back_one,
    back_two,
    back_three,
    halo,
    source_weight,
    dest_weight,
    totals,
    dest,
    table,
    dest_parts,
    picked_one,
    picked_two,
):
    rows, width = own.shape
    project(table, (own, back_one, back_two, back_three, halo), source_weight)
    dest[...] = mm(own[...], dest_weight[...])
    split_dest(dest[:, :width], dest_parts)
    totals[...] = jnp.zeros_like(totals)
    limit = 4 * rows + halo.shape[0]
    chunks = (0, (jnp.maximum(near_count[0], near_count[1]) + CHUNK - 1) // CHUNK)
    picked = (picked_one, picked_two)
    add_edges(chunks, 0, limit, keys, key_col, key_row, table, dest_parts, picked, totals)


def far_kernel(
    keys,
    near_count,
    key_col,
    key_row,
    halo_one,
    halo_two,
    halo_three,
    source_weight,
    near_totals,
    dest,
    own,
    norm_gain,
    router_weight,
    routes,
    slot_row,
    cotangent,
    graph_out,
    weight_first,
    send,
    table,
    dest_parts,
    picked_one,
    picked_two,
    totals,
):
    rows, width = own.shape
    project(table, (halo_one, halo_two, halo_three), source_weight)
    split_dest(dest[:, :width], dest_parts)
    totals[...] = near_totals[...]
    base = 4 * rows + halo_one.shape[0]
    limit = base + 3 * halo_one.shape[0]
    chunks = (jnp.minimum(near_count[0], near_count[1]) // CHUNK, keys.shape[1] // CHUNK)
    picked = (picked_one, picked_two)
    add_edges(chunks, base, limit, keys, key_col, key_row, table, dest_parts, picked, totals)

    whole = totals[...].reshape(rows, 2 * width)
    agg = whole[:, :width] / jnp.maximum(whole[:, width:], 1.0)
    pre_norm = dest[:, width:] + agg
    average = jnp.mean(pre_norm, axis=1, keepdims=True)
    center = pre_norm - average
    variance = jnp.mean(center * center, axis=1, keepdims=True)
    normed = center * lax.rsqrt(variance + 1e-05) * norm_gain[...]
    result = (own[...].astype(F32) + jnp.maximum(normed, 0.0)).astype(BF16)
    graph_out[...] = result

    logits = mm(result, router_weight[...])
    gap_mask = hit_gap(routes, logits.shape)
    first_weight = jax.nn.sigmoid(jnp.sum(logits * gap_mask, axis=1, keepdims=True))
    weight_first[...] = first_weight
    cot = cotangent[...].astype(F32)
    grads_first = (first_weight * cot).astype(BF16)
    grads_second = ((1.0 - first_weight) * cot).astype(BF16)
    experts = router_weight.shape[1]
    capacity = send.shape[1] // PANELS
    slot = sublanes((experts * capacity, rows))
    to_first = one_hot(slot_row[0:1, :] == slot)
    to_second = one_hot(slot_row[1:2, :] == slot)
    rows_out = mm(to_first + to_second, result).astype(BF16)
    grads_out = (mm(to_first, grads_first) + mm(to_second, grads_second)).astype(BF16)
    about_first = about(1.0 - first_weight, routes[:, 1:2])
    about_second = about(first_weight, routes[:, 0:1])
    about_out = (mm(to_first, about_first) + mm(to_second, about_second)).astype(BF16)
    panels = [v[:, i : i + 128] for v in (rows_out, grads_out) for i in range(0, width, 128)]
    for p, panel in enumerate(panels + [about_out]):
        send[:, p * capacity : (p + 1) * capacity] = panel.reshape(experts, capacity, 128)


def about(weight, expert):
    high = weight.astype(BF16).astype(F32)
    lane = lanes((weight.shape[0], 128))
    parts = jnp.where(lane == 0, high, jnp.where(lane == 1, weight - high, 0.0))
    return jnp.where(lane == 2, expert.astype(F32), parts).astype(BF16)


def hit_gap(routes, shape):
    spot = lanes(shape)
    first = jnp.where(routes[:, 0:1] == spot, 1.0, 0.0)
    second = jnp.where(routes[:, 1:2] == spot, 1.0, 0.0)
    return first - second


def unpack(arrived, chunks, capacity, start, count):
    parts = [
        arrived[chunks, p * capacity : (p + 1) * capacity].reshape(-1, 128)
        for p in range(start, start + count)
    ]
    return jnp.concatenate(parts, axis=1)


def store(back, chunks, capacity, rows):
    for p in range(rows.shape[1] // 128):
        panel = rows[:, p * 128 : (p + 1) * 128]
        back[chunks, p * capacity : (p + 1) * capacity] = panel.reshape(-1, capacity, 128)


def forward_kernel(expert, arrived, *refs):
    ins, outs, back, router_sum = refs[:4], refs[4:8], refs[8], refs[9]
    capacity = arrived.shape[1] // PANELS
    step = CHUNK // capacity
    experts = router_sum.shape[0]
    router_sum[...] = jnp.zeros_like(router_sum)

    def block(b, carry):
        chunks = pl.ds(b * step, step)
        rows = unpack(arrived, chunks, capacity, 0, 4)
        grads = unpack(arrived, chunks, capacity, 4, 4)
        other = unpack(arrived, chunks, capacity, 8, 1).astype(F32)
        y = None
        for w_in, w_out in zip(ins, outs):
            x = mm(rows, w_in[...])
            tanh = jnp.tanh(x * (0.7978845608028654 + 0.035677408136300125 * (x * x)))
            part = mm((x * (0.5 + 0.5 * tanh)).astype(BF16), w_out[...])
            y = part if y is None else y + part
        store(back, chunks, capacity, y.astype(BF16))
        share = jnp.sum(grads.astype(F32) * y, axis=1, keepdims=True)
        share = share * (other[:, 0:1] + other[:, 1:2])
        lane = lanes((CHUNK, experts))
        own_lane = jnp.where(lane == expert[0], 1.0, 0.0)
        other_lane = jnp.where(lane.astype(F32) == other[:, 2:3], 1.0, 0.0)
        shares = share * (own_lane - other_lane)
        high = shares.astype(BF16)
        low = (shares - high.astype(F32)).astype(BF16)
        both = mm(jnp.concatenate([high, low], axis=1), rows, ((0,), (0,)))
        router_sum[...] += both[:experts] + both[experts:]
        return carry

    lax.fori_loop(0, arrived.shape[0] // step, block, 0)
    spot = lax.broadcasted_iota(I32, (experts, capacity, 128), 1)
    tile = jnp.zeros((experts, capacity, 128), F32)
    for i in range(4):
        part = router_sum[:, i * 128 : (i + 1) * 128]
        high = part.astype(BF16).astype(F32)
        tile = jnp.where(spot == i, high[:, None, :], tile)
        tile = jnp.where(spot == 4 + i, (part - high)[:, None, :], tile)
    back[:, 4 * capacity :] = tile.astype(BF16)


def backward_kernel(arrived, *refs):
    ins, outs, back = refs[:4], refs[4:8], refs[8]
    blocks, act_all, hidden_all = refs[9:18], refs[18], refs[19]
    capacity = arrived.shape[1] // PANELS
    step = CHUNK // capacity

    def block(b, carry):
        at = pl.ds(pl.multiple_of(b * CHUNK, CHUNK), CHUNK)
        chunks = pl.ds(b * step, step)
        rows = unpack(arrived, chunks, capacity, 0, 4)
        grads = unpack(arrived, chunks, capacity, 4, 4)
        dx = None
        for s, (w_in, w_out) in enumerate(zip(ins, outs)):
            x = mm(rows, w_in[...])
            square = x * x
            tanh = jnp.tanh(x * (0.7978845608028654 + 0.035677408136300125 * square))
            half = 0.5 + 0.5 * tanh
            slope = 0.7978845608028654 + 0.10703222440890037 * square
            back_slope = half + 0.5 * x * (1.0 - tanh * tanh) * slope
            hidden = (back_slope * mm(grads, w_out[...], ((1,), (1,)))).astype(BF16)
            act_all[s, at, :] = (x * half).astype(BF16)
            hidden_all[s, at, :] = hidden
            part = mm(hidden, w_in[...], ((1,), (1,)))
            dx = part if dx is None else dx + part
        store(back, chunks, capacity, dx.astype(BF16))
        return carry

    lax.fori_loop(0, arrived.shape[0] // step, block, 0)
    back[:, 4 * capacity :] = jnp.zeros((back.shape[0], capacity, 128), BF16)
    rows = unpack(arrived, slice(None), capacity, 0, 4)
    grads = unpack(arrived, slice(None), capacity, 4, 4)
    for s in range(4):
        grad_in = mm(rows, hidden_all[s], ((0,), (0,))).astype(BF16)
        grad_out = mm(act_all[s], grads, ((0,), (0,))).astype(BF16)
        if s == 2:
            blocks[2][...] = blocks[6][...] = jnp.zeros((8, 128), BF16)
            pack(blocks[8], grad_in, grad_out)
        else:
            blocks[s][...] = grad_in
            blocks[4 + s][...] = grad_out


def pack(block, *parts):
    at = 0
    for part in parts:
        for i in range(0, part.shape[1], 128):
            block[at : at + part.shape[0]] = part[:, i : i + 128]
            at += part.shape[0]


def output_kernel(back, slot_col, graph_out, weight_first, cotangent, layer_out, gap_grad):
    rows, width = graph_out.shape
    capacity = back.shape[1] // 5
    slot = lanes((rows, back.shape[0] * capacity))
    y = unpack(back, slice(None), capacity, 0, 4)
    first = mm(one_hot(slot_col[:, 0:1] == slot), y)
    second = mm(one_hot(slot_col[:, 1:2] == slot), y)
    one, two = weight_first[...], 1.0 - weight_first[...]
    layer_out[...] = (graph_out[...].astype(F32) + (one * first + two * second)).astype(BF16)
    cot = cotangent[...].astype(F32)
    gap_grad[...] = jnp.sum(cot * (first - second), axis=1, keepdims=True) * one * two


def input_kernel(back, slot_col, gap_grad, weight_first, cotangent, routes, router_t, grad):
    capacity = back.shape[1] // 5
    rows = cotangent.shape[0]
    slot = lanes((rows, back.shape[0] * capacity))
    dx = unpack(back, slice(None), capacity, 0, 4)
    one, two = weight_first[...], 1.0 - weight_first[...]
    mixed = one * mm(one_hot(slot_col[:, 0:1] == slot), dx)
    mixed = mixed + two * mm(one_hot(slot_col[:, 1:2] == slot), dx)
    spread = mm(hit_gap(routes, (rows, router_t.shape[0])).astype(BF16), router_t[...])
    grad[...] = cotangent[...].astype(F32) + mixed + gap_grad[...] * spread


def halo_kernel(list_col, node_feats, send):
    pick = one_hot(list_col[...] == lanes((list_col.shape[0], node_feats.shape[0])))
    send[...] = mm(pick, node_feats[...]).astype(BF16).reshape(send.shape)


def hold(values):
    return lax.optimization_barrier(values)


def ring(n, s):
    return [(i, (i + s) % n) for i in range(n)]


def on_device(
    node_feats,
    halo_rows,
    edge_src,
    edge_dst,
    dest_weight,
    source_weight,
    norm_gain,
    router_weight,
    routes,
    expert_in,
    expert_out,
    cotangent,
):
    rows, width = node_feats.shape
    wide_count = lax.axis_size("wide")
    narrow_count = lax.axis_size("hi") * lax.axis_size("lo")
    my_lo = lax.axis_index("lo")
    me = lax.axis_index("hi") * 2 + my_lo
    peer = halo_rows.shape[-1]
    part_rows = narrow_count * rows
    experts = router_weight.shape[1]
    capacity = 4 * rows // experts
    tiles, slots = edge_src.shape

    def around(value, s):
        return lax.ppermute(value, NARROW, ring(narrow_count, s))

    def weight_to(weight, s):
        which = (my_lo + s) % 2
        return lax.dynamic_index_in_dim(weight, which, 0, keepdims=False)

    in_blocks = [weight_to(expert_in, 0)] + [None] * 3
    out_blocks = [weight_to(expert_out, 0)] + [None] * 3

    per_narrow = wide_count * peer
    local = edge_src < part_rows
    halo_id = edge_src - part_rows
    size = jnp.where(local, rows, per_narrow)
    offset = jnp.where(local, edge_src, halo_id)
    place = (me - offset // size) % narrow_count * size + offset % size
    place = place + jnp.where(local, 0, part_rows)
    keys = place * 256 + edge_dst

    halo_send = call(
        halo_kernel,
        array((wide_count, peer, width), BF16),
        (halo_rows.reshape(-1, 1), node_feats),
    )
    keys = lax.sort(keys, dimension=1)
    near_rows = part_rows + per_narrow
    near_count = jnp.sum((keys < near_rows * 256).astype(I32), axis=1)
    key_col = keys.reshape(tiles, slots, 1)
    key_row = keys.reshape(tiles, 1, slots)
    received = lax.all_to_all(halo_send, "wide", split_axis=0, concat_axis=0, tiled=True)
    received = received.reshape(-1, width)
    parts = [node_feats] + [around(node_feats, s) for s in range(1, narrow_count)]
    for s in EARLY_IN:
        in_blocks[s] = around(weight_to(expert_in, s), s)
    received, parts, in_blocks, keys, key_col, key_row, near_count = hold(
        (received, parts, in_blocks, keys, key_col, key_row, near_count)
    )
    halos = [received] + [around(received, s) for s in range(1, narrow_count)]

    route_rows = routes.T.reshape(-1)
    hits = (route_rows[:, None] == jnp.arange(experts, dtype=I32)[None, :]).astype(BF16)
    pair_ids = jnp.arange(2 * rows, dtype=I32)
    earlier = (pair_ids[None, :] < pair_ids[:, None]).astype(BF16)
    ahead = jnp.dot(earlier, hits, preferred_element_type=F32)
    position = jnp.sum(ahead * hits.astype(F32), axis=1).astype(I32)
    slot_row = (route_rows * capacity + position).reshape(2, rows)
    slot_col = slot_row.T

    near_totals, dest = call(
        near_kernel,
        (array((tiles, TILE, 2 * width), F32), array((rows, 2 * width), F32)),
        (keys, near_count, key_col, key_row, *parts, halos[0], source_weight, dest_weight),
        scratch=(
            pltpu.VMEM((near_rows + WINDOW, 2 * width), BF16),
            pltpu.VMEM((tiles, 2 * TILE, width), BF16),
            pltpu.VMEM((CHUNK, 2 * width), F32),
            pltpu.VMEM((CHUNK, 2 * width), F32),
        ),
        smem=(0, 1),
        cost=14,
    )
    halos, near_totals, expert_in, expert_out = hold((halos, near_totals, expert_in, expert_out))
    for s in range(1, narrow_count):
        if s not in EARLY_IN:
            in_blocks[s] = around(weight_to(expert_in, s), s)
        out_blocks[s] = around(weight_to(expert_out, s), s)
    graph_out, weight_first, send = call(
        far_kernel,
        (
            array((rows, width), BF16),
            array((rows, 1), F32),
            array((experts, PANELS * capacity, 128), BF16),
        ),
        (
            keys,
            near_count,
            key_col,
            key_row,
            *halos[1:],
            source_weight,
            near_totals,
            dest,
            node_feats,
            norm_gain.reshape(1, width),
            router_weight,
            routes,
            slot_row,
            cotangent,
        ),
        scratch=(
            pltpu.VMEM((3 * per_narrow + WINDOW, 2 * width), BF16),
            pltpu.VMEM((tiles, 2 * TILE, width), BF16),
            pltpu.VMEM((CHUNK, 2 * width), F32),
            pltpu.VMEM((CHUNK, 2 * width), F32),
            pltpu.VMEM((tiles, TILE, 2 * width), F32),
        ),
        smem=(0, 1),
        cost=18,
    )
    sooner = [in_blocks[s] for s in SOON_IN] + [out_blocks[s] for s in SOON_OUT]
    send, sooner = hold((send, sooner))
    for s, block in zip(SOON_IN, sooner):
        in_blocks[s] = block
    for s, block in zip(SOON_OUT, sooner[len(SOON_IN) :]):
        out_blocks[s] = block
    arrived = lax.all_to_all(send, OWNERS, split_axis=0, concat_axis=0, tiled=True)
    blocks = in_blocks + out_blocks
    hidden_block = expert_in.shape[2]
    expert = (lax.axis_index("wide") * 2 + my_lo).astype(I32).reshape(1)
    saved = pltpu.VMEM((4, experts * capacity, hidden_block), BF16)
    packed = array((experts, 5 * capacity, 128), BF16)
    back_y = call(
        forward_kernel,
        packed,
        (expert, arrived, *blocks),
        scratch=(pltpu.VMEM((experts, width), F32),),
        smem=(0,),
        cost=8,
    )
    grad_shapes = [array((width, hidden_block), BF16)] * 4 + [array((hidden_block, width), BF16)] * 4
    grad_shapes[2] = grad_shapes[6] = array((8, 128), BF16)
    grad_shapes.append(array((2 * width * hidden_block // 128, 128), BF16))
    back_dx, *grad_blocks = call(
        backward_kernel, (packed, *grad_shapes), (arrived, *blocks), scratch=(saved, saved), cost=12
    )

    arrivals = [around(grad_blocks[i], -s) for i, s in ((1, 1), (3, 3), (5, 1), (7, 3), (8, 2))]

    def home(back):
        mine = back[0].astype(F32) + back[2].astype(F32)
        other = back[1].astype(F32) + back[3].astype(F32)
        low = my_lo == 0
        return jnp.stack([jnp.where(low, mine, other), jnp.where(low, other, mine)])

    def swap(back):
        return lax.all_to_all(back, OWNERS, split_axis=0, concat_axis=0, tiled=True)

    at = 4 * capacity
    back_y = swap(back_y)
    pieces = back_y[:, at : at + 8].astype(F32).reshape(experts, 2, 4, 128)
    piece = jnp.sum(pieces, axis=(0, 1))
    high = piece.astype(BF16)
    low = (piece - high.astype(F32)).astype(BF16)
    panel = jnp.concatenate([high, low, jnp.zeros((capacity - 8, 128), BF16)], axis=0)
    back_dx = lax.dynamic_update_slice(
        back_dx, jnp.broadcast_to(panel[None], (experts, capacity, 128)), (0, at, 0)
    )
    back_dx = swap(back_dx)
    layer_out, gap_grad = call(
        output_kernel,
        (array((rows, width), BF16), array((rows, 1), F32)),
        (back_y, slot_col, graph_out, weight_first, cotangent),
        cost=3,
    )
    gap_grad, arrivals = hold((gap_grad, arrivals))
    in_one, in_three, out_one, out_three, both = arrivals
    in_two = jnp.concatenate([both[:width], both[width : 2 * width]], axis=1)
    starts = range(2 * width, 4 * width, hidden_block)
    out_two = jnp.concatenate([both[i : i + hidden_block] for i in starts], axis=1)
    in_back = (grad_blocks[0], in_one, in_two, in_three)
    out_back = (grad_blocks[4], out_one, out_two, out_three)
    sums = back_dx[:, at : at + 8].astype(F32).reshape(experts, 2, width)
    sums = sums[:, 0] + sums[:, 1]
    router_total = sums + lax.ppermute(sums, "hi", [(0, 1), (1, 0)])
    grad_features = call(
        input_kernel,
        array((rows, width), F32),
        (back_dx, slot_col, gap_grad, weight_first, cotangent, routes, router_weight.T),
        cost=2,
    )
    grad_expert_in = home(in_back)
    grad_expert_out = home(out_back)
    grad_router = router_total.T
    return (layer_out, grad_features, grad_expert_in, grad_expert_out, grad_router)


def solution(mesh):
    wide_count, narrow_count = mesh.devices.shape
    fine = Mesh(mesh.devices.reshape(wide_count, narrow_count // 2, 2), ALL)
    placed = (
        P(ALL, None),
        P("wide", NARROW, None, None),
        P(ALL, None),
        P(ALL, None),
        P(),
        P(),
        P(),
        P(),
        P(ALL, None),
        P("wide", None, NARROW),
        P("wide", NARROW, None),
        P(ALL, None),
    )
    return jax.shard_map(
        on_device,
        mesh=fine,
        in_specs=placed,
        out_specs=(
            P(ALL, None),
            P(ALL, None),
            P("wide", None, NARROW),
            P("wide", NARROW, None),
            P(),
        ),
        check_vma=False,
    )
```

```python
import jax
import jax.numpy as jnp
from jax import lax
from jax.experimental import pallas as pl
from jax.experimental.pallas import tpu as pltpu
from jax.sharding import Mesh
from jax.sharding import PartitionSpec as P

TILE = 128
CHUNK = 256
WINDOW = 512
PANELS = 9
ALL = ("wide", "hi", "lo")
NARROW = ("hi", "lo")
OWNERS = ("wide", "lo")
F32 = jnp.float32
BF16 = jnp.bfloat16
I32 = jnp.int32
EARLY_IN = (1, 3)
SOON_IN = (2,)
SOON_OUT = (1, 3)
FLOPS_PER_US = 10**9
BYTES_PER_US = 3 * 10**6
VMEM_LIMIT = 52 * 1024 * 1024


def mm(a, b, over=((1,), (0,))):
    return lax.dot_general(a, b, (over, ((), ())), preferred_element_type=F32)


def lanes(shape):
    return lax.broadcasted_iota(I32, shape, len(shape) - 1)


def sublanes(shape):
    return lax.broadcasted_iota(I32, shape, len(shape) - 2)


def one_hot(hit):
    return jnp.where(hit, 1.0, 0.0).astype(BF16)


def call(kernel, outs, args, scratch=(), smem=(), cost=1):
    in_specs = [
        pl.BlockSpec(memory_space=pltpu.SMEM if i in smem else pltpu.VMEM) for i in range(len(args))
    ]
    return pl.pallas_call(
        kernel,
        out_shape=outs,
        in_specs=in_specs,
        out_specs=jax.tree.map(lambda _: pl.BlockSpec(memory_space=pltpu.VMEM), outs),
        scratch_shapes=list(scratch),
        compiler_params=pltpu.CompilerParams(vmem_limit_bytes=VMEM_LIMIT),
        cost_estimate=pl.CostEstimate(
            flops=cost * FLOPS_PER_US, transcendentals=0, bytes_accessed=cost * BYTES_PER_US
        ),
    )(*args)


def array(shape, dtype):
    return jax.ShapeDtypeStruct(shape, dtype)


def project(table, parts, weight):
    at = 0
    for part in parts:
        for start in range(0, part.shape[0], CHUNK):
            rows = mm(part[start : start + CHUNK], weight[...])
            table[at : at + CHUNK] = rows.astype(BF16)
            at += CHUNK
    table[at:] = jnp.zeros((WINDOW, table.shape[1]), BF16)


def split_dest(dest, dest_parts):
    high = dest.astype(BF16)
    low = (dest - high.astype(F32)).astype(BF16)
    for t in range(dest_parts.shape[0]):
        dest_parts[t, :TILE] = high[t * TILE : (t + 1) * TILE]
        dest_parts[t, TILE:] = low[t * TILE : (t + 1) * TILE]


def add_edges(chunks, base, limit, keys, key_col, key_row, table, dest_parts, picked, totals):
    width = dest_parts.shape[2]
    spot = lanes((CHUNK, WINDOW))
    tile_spot = lanes((CHUNK, 2 * TILE)) & (TILE - 1)

    def gather(t, c, k):
        first = jnp.clip((keys[t, c * CHUNK] >> 8) - base, 0, limit - base) & ~15
        at = pl.multiple_of(first + k * WINDOW, 16)
        key = key_col[t, pl.ds(pl.multiple_of(c * CHUNK, CHUNK), CHUNK), :]
        row = (key >> 8) - (base + at)
        return mm(one_hot(row == spot), table[pl.ds(at, WINDOW), :])

    def more(t, c):
        first = jnp.clip((keys[t, c * CHUNK] >> 8) - base, 0, limit - base) & ~15
        last = jnp.minimum(keys[t, c * CHUNK + CHUNK - 1] >> 8, limit - 1) - base

        def window(k, carry):
            picked[t][...] += gather(t, c, k)
            return carry

        lax.fori_loop(1, (jnp.maximum(last - first, 0) >> 9) + 1, window, 0)

    def add(t, c, live):
        start = pl.multiple_of(c * CHUNK, CHUNK)
        key = key_col[t, pl.ds(start, CHUNK), :]
        dest_gate = mm(one_hot((key & 255) == tile_spot), dest_parts[t])
        pre = picked[t][:, :width] + dest_gate
        gates = (0.5 * jnp.tanh(0.5 * pre) + 0.5).astype(BF16)
        messages = gates * picked[t][:, width:].astype(BF16)
        row_key = key_row[t, :, pl.ds(start, CHUNK)]
        source = row_key >> 8
        target = jnp.where((source >= base) & (source < limit) & live, row_key & 255, 255)
        selector = one_hot(target == sublanes((TILE, CHUNK)))
        totals[t, :, :width] += mm(selector, messages)
        totals[t, :, width:] += mm(selector, gates)

    picked[1][...] = jnp.zeros_like(picked[1])
    begin, end = chunks

    def both(c, carry):
        picked[0][...] = gather(0, c, 0)
        add(1, jnp.maximum(c - 1, 0), c > begin)
        more(0, c)
        picked[1][...] = gather(1, c, 0)
        add(0, c, c >= begin)
        more(1, c)
        return carry

    lax.fori_loop(begin, end, both, 0)
    add(1, jnp.maximum(end - 1, 0), end > begin)


def near_kernel(
    keys,
    near_count,
    key_col,
    key_row,
    own,
    back_one,
    back_two,
    back_three,
    halo,
    source_weight,
    dest_weight,
    totals,
    dest,
    table,
    dest_parts,
    picked_one,
    picked_two,
):
    rows, width = own.shape
    project(table, (own, back_one, back_two, back_three, halo), source_weight)
    dest[...] = mm(own[...], dest_weight[...])
    split_dest(dest[:, :width], dest_parts)
    totals[...] = jnp.zeros_like(totals)
    limit = 4 * rows + halo.shape[0]
    chunks = (0, (jnp.maximum(near_count[0], near_count[1]) + CHUNK - 1) // CHUNK)
    picked = (picked_one, picked_two)
    add_edges(chunks, 0, limit, keys, key_col, key_row, table, dest_parts, picked, totals)


def far_kernel(
    keys,
    near_count,
    key_col,
    key_row,
    halo_one,
    halo_two,
    halo_three,
    source_weight,
    near_totals,
    dest,
    own,
    norm_gain,
    router_weight,
    routes,
    slot_row,
    cotangent,
    graph_out,
    weight_first,
    send,
    table,
    dest_parts,
    picked_one,
    picked_two,
    totals,
):
    rows, width = own.shape
    project(table, (halo_one, halo_two, halo_three), source_weight)
    split_dest(dest[:, :width], dest_parts)
    totals[...] = near_totals[...]
    base = 4 * rows + halo_one.shape[0]
    limit = base + 3 * halo_one.shape[0]
    chunks = (jnp.minimum(near_count[0], near_count[1]) // CHUNK, keys.shape[1] // CHUNK)
    picked = (picked_one, picked_two)
    add_edges(chunks, base, limit, keys, key_col, key_row, table, dest_parts, picked, totals)

    whole = totals[...].reshape(rows, 2 * width)
    agg = whole[:, :width] / jnp.maximum(whole[:, width:], 1.0)
    pre_norm = dest[:, width:] + agg
    average = jnp.mean(pre_norm, axis=1, keepdims=True)
    center = pre_norm - average
    variance = jnp.mean(center * center, axis=1, keepdims=True)
    normed = center * lax.rsqrt(variance + 1e-05) * norm_gain[...]
    result = (own[...].astype(F32) + jnp.maximum(normed, 0.0)).astype(BF16)
    graph_out[...] = result

    logits = mm(result, router_weight[...])
    gap_mask = hit_gap(routes, logits.shape)
    first_weight = jax.nn.sigmoid(jnp.sum(logits * gap_mask, axis=1, keepdims=True))
    weight_first[...] = first_weight
    cot = cotangent[...].astype(F32)
    grads_first = (first_weight * cot).astype(BF16)
    grads_second = ((1.0 - first_weight) * cot).astype(BF16)
    experts = router_weight.shape[1]
    capacity = send.shape[1] // PANELS
    slot = sublanes((experts * capacity, rows))
    to_first = one_hot(slot_row[0:1, :] == slot)
    to_second = one_hot(slot_row[1:2, :] == slot)
    rows_out = mm(to_first + to_second, result).astype(BF16)
    grads_out = (mm(to_first, grads_first) + mm(to_second, grads_second)).astype(BF16)
    about_first = about(1.0 - first_weight, routes[:, 1:2])
    about_second = about(first_weight, routes[:, 0:1])
    about_out = (mm(to_first, about_first) + mm(to_second, about_second)).astype(BF16)
    panels = [v[:, i : i + 128] for v in (rows_out, grads_out) for i in range(0, width, 128)]
    for p, panel in enumerate(panels + [about_out]):
        send[:, p * capacity : (p + 1) * capacity] = panel.reshape(experts, capacity, 128)


def about(weight, expert):
    high = weight.astype(BF16).astype(F32)
    lane = lanes((weight.shape[0], 128))
    parts = jnp.where(lane == 0, high, jnp.where(lane == 1, weight - high, 0.0))
    return jnp.where(lane == 2, expert.astype(F32), parts).astype(BF16)


def hit_gap(routes, shape):
    spot = lanes(shape)
    first = jnp.where(routes[:, 0:1] == spot, 1.0, 0.0)
    second = jnp.where(routes[:, 1:2] == spot, 1.0, 0.0)
    return first - second


def unpack(arrived, chunks, capacity, start, count):
    parts = [
        arrived[chunks, p * capacity : (p + 1) * capacity].reshape(-1, 128)
        for p in range(start, start + count)
    ]
    return jnp.concatenate(parts, axis=1)


def store(back, chunks, capacity, rows):
    for p in range(rows.shape[1] // 128):
        panel = rows[:, p * 128 : (p + 1) * 128]
        back[chunks, p * capacity : (p + 1) * capacity] = panel.reshape(-1, capacity, 128)


def forward_kernel(expert, arrived, *refs):
    ins, outs, back, router_sum = refs[:4], refs[4:8], refs[8], refs[9]
    capacity = arrived.shape[1] // PANELS
    step = CHUNK // capacity
    experts = router_sum.shape[0]
    router_sum[...] = jnp.zeros_like(router_sum)

    def block(b, carry):
        chunks = pl.ds(b * step, step)
        rows = unpack(arrived, chunks, capacity, 0, 4)
        grads = unpack(arrived, chunks, capacity, 4, 4)
        other = unpack(arrived, chunks, capacity, 8, 1).astype(F32)
        y = None
        for w_in, w_out in zip(ins, outs):
            x = mm(rows, w_in[...])
            tanh = jnp.tanh(x * (0.7978845608028654 + 0.035677408136300125 * (x * x)))
            part = mm((x * (0.5 + 0.5 * tanh)).astype(BF16), w_out[...])
            y = part if y is None else y + part
        store(back, chunks, capacity, y.astype(BF16))
        share = jnp.sum(grads.astype(F32) * y, axis=1, keepdims=True)
        share = share * (other[:, 0:1] + other[:, 1:2])
        lane = lanes((CHUNK, experts))
        own_lane = jnp.where(lane == expert[0], 1.0, 0.0)
        other_lane = jnp.where(lane.astype(F32) == other[:, 2:3], 1.0, 0.0)
        shares = share * (own_lane - other_lane)
        high = shares.astype(BF16)
        low = (shares - high.astype(F32)).astype(BF16)
        both = mm(jnp.concatenate([high, low], axis=1), rows, ((0,), (0,)))
        router_sum[...] += both[:experts] + both[experts:]
        return carry

    lax.fori_loop(0, arrived.shape[0] // step, block, 0)
    spot = lax.broadcasted_iota(I32, (experts, capacity, 128), 1)
    tile = jnp.zeros((experts, capacity, 128), F32)
    for i in range(4):
        part = router_sum[:, i * 128 : (i + 1) * 128]
        high = part.astype(BF16).astype(F32)
        tile = jnp.where(spot == i, high[:, None, :], tile)
        tile = jnp.where(spot == 4 + i, (part - high)[:, None, :], tile)
    back[:, 4 * capacity :] = tile.astype(BF16)


def backward_kernel(arrived, *refs):
    ins, outs, back = refs[:4], refs[4:8], refs[8]
    blocks, act_all, hidden_all = refs[9:18], refs[18], refs[19]
    capacity = arrived.shape[1] // PANELS
    step = CHUNK // capacity

    def block(b, carry):
        at = pl.ds(pl.multiple_of(b * CHUNK, CHUNK), CHUNK)
        chunks = pl.ds(b * step, step)
        rows = unpack(arrived, chunks, capacity, 0, 4)
        grads = unpack(arrived, chunks, capacity, 4, 4)
        dx = None
        for s, (w_in, w_out) in enumerate(zip(ins, outs)):
            x = mm(rows, w_in[...])
            square = x * x
            tanh = jnp.tanh(x * (0.7978845608028654 + 0.035677408136300125 * square))
            half = 0.5 + 0.5 * tanh
            slope = 0.7978845608028654 + 0.10703222440890037 * square
            back_slope = half + 0.5 * x * (1.0 - tanh * tanh) * slope
            hidden = (back_slope * mm(grads, w_out[...], ((1,), (1,)))).astype(BF16)
            act_all[s, at, :] = (x * half).astype(BF16)
            hidden_all[s, at, :] = hidden
            part = mm(hidden, w_in[...], ((1,), (1,)))
            dx = part if dx is None else dx + part
        store(back, chunks, capacity, dx.astype(BF16))
        return carry

    lax.fori_loop(0, arrived.shape[0] // step, block, 0)
    back[:, 4 * capacity :] = jnp.zeros((back.shape[0], capacity, 128), BF16)
    rows = unpack(arrived, slice(None), capacity, 0, 4)
    grads = unpack(arrived, slice(None), capacity, 4, 4)
    for s in range(4):
        grad_in = mm(rows, hidden_all[s], ((0,), (0,))).astype(BF16)
        grad_out = mm(act_all[s], grads, ((0,), (0,))).astype(BF16)
        if s == 2:
            blocks[2][...] = blocks[6][...] = jnp.zeros((8, 128), BF16)
            pack(blocks[8], grad_in, grad_out)
        else:
            blocks[s][...] = grad_in
            blocks[4 + s][...] = grad_out


def pack(block, *parts):
    at = 0
    for part in parts:
        for i in range(0, part.shape[1], 128):
            block[at : at + part.shape[0]] = part[:, i : i + 128]
            at += part.shape[0]


def home_kernel(
    my_lo, own_in, own_out, in_one, in_three, out_one, out_three, two, grad_in, grad_out
):
    lo = my_lo[0]
    width, hidden = own_in.shape
    in_two = jnp.concatenate([two[:width], two[width : 2 * width]], axis=1)
    starts = range(2 * width, 4 * width, hidden)
    out_two = jnp.concatenate([two[i : i + hidden] for i in starts], axis=1)
    grad_in[lo] = own_in[...].astype(F32) + in_two.astype(F32)
    grad_out[lo] = own_out[...].astype(F32) + out_two.astype(F32)
    grad_in[1 - lo] = in_one[...].astype(F32) + in_three[...].astype(F32)
    grad_out[1 - lo] = out_one[...].astype(F32) + out_three[...].astype(F32)


def output_kernel(back, slot_col, graph_out, weight_first, cotangent, layer_out, gap_grad):
    rows, width = graph_out.shape
    capacity = back.shape[1] // 5
    slot = lanes((rows, back.shape[0] * capacity))
    y = unpack(back, slice(None), capacity, 0, 4)
    first = mm(one_hot(slot_col[:, 0:1] == slot), y)
    second = mm(one_hot(slot_col[:, 1:2] == slot), y)
    one, two = weight_first[...], 1.0 - weight_first[...]
    layer_out[...] = (graph_out[...].astype(F32) + (one * first + two * second)).astype(BF16)
    cot = cotangent[...].astype(F32)
    gap_grad[...] = jnp.sum(cot * (first - second), axis=1, keepdims=True) * one * two


def input_kernel(back, slot_col, gap_grad, weight_first, cotangent, routes, router_t, grad):
    capacity = back.shape[1] // 5
    rows = cotangent.shape[0]
    slot = lanes((rows, back.shape[0] * capacity))
    dx = unpack(back, slice(None), capacity, 0, 4)
    one, two = weight_first[...], 1.0 - weight_first[...]
    mixed = one * mm(one_hot(slot_col[:, 0:1] == slot), dx)
    mixed = mixed + two * mm(one_hot(slot_col[:, 1:2] == slot), dx)
    spread = mm(hit_gap(routes, (rows, router_t.shape[0])).astype(BF16), router_t[...])
    grad[...] = cotangent[...].astype(F32) + mixed + gap_grad[...] * spread


def halo_kernel(list_col, node_feats, send):
    pick = one_hot(list_col[...] == lanes((list_col.shape[0], node_feats.shape[0])))
    send[...] = mm(pick, node_feats[...]).astype(BF16).reshape(send.shape)


def hold(values):
    return lax.optimization_barrier(values)


def ring(n, s):
    return [(i, (i + s) % n) for i in range(n)]


def on_device(
    node_feats,
    halo_rows,
    edge_src,
    edge_dst,
    dest_weight,
    source_weight,
    norm_gain,
    router_weight,
    routes,
    expert_in,
    expert_out,
    cotangent,
):
    rows, width = node_feats.shape
    wide_count = lax.axis_size("wide")
    narrow_count = lax.axis_size("hi") * lax.axis_size("lo")
    my_lo = lax.axis_index("lo")
    me = lax.axis_index("hi") * 2 + my_lo
    peer = halo_rows.shape[-1]
    part_rows = narrow_count * rows
    experts = router_weight.shape[1]
    capacity = 4 * rows // experts
    tiles, slots = edge_src.shape

    def around(value, s):
        return lax.ppermute(value, NARROW, ring(narrow_count, s))

    def weight_to(weight, s):
        which = (my_lo + s) % 2
        return lax.dynamic_index_in_dim(weight, which, 0, keepdims=False)

    in_blocks = [weight_to(expert_in, 0)] + [None] * 3
    out_blocks = [weight_to(expert_out, 0)] + [None] * 3

    per_narrow = wide_count * peer
    local = edge_src < part_rows
    halo_id = edge_src - part_rows
    size = jnp.where(local, rows, per_narrow)
    offset = jnp.where(local, edge_src, halo_id)
    place = (me - offset // size) % narrow_count * size + offset % size
    place = place + jnp.where(local, 0, part_rows)
    keys = place * 256 + edge_dst

    halo_send = call(
        halo_kernel,
        array((wide_count, peer, width), BF16),
        (halo_rows.reshape(-1, 1), node_feats),
    )
    keys = lax.sort(keys, dimension=1)
    near_rows = part_rows + per_narrow
    near_count = jnp.sum((keys < near_rows * 256).astype(I32), axis=1)
    key_col = keys.reshape(tiles, slots, 1)
    key_row = keys.reshape(tiles, 1, slots)
    received = lax.all_to_all(halo_send, "wide", split_axis=0, concat_axis=0, tiled=True)
    received = received.reshape(-1, width)
    parts = [node_feats] + [around(node_feats, s) for s in range(1, narrow_count)]
    for s in EARLY_IN:
        in_blocks[s] = around(weight_to(expert_in, s), s)
    received, parts, in_blocks, keys, key_col, key_row, near_count = hold(
        (received, parts, in_blocks, keys, key_col, key_row, near_count)
    )
    halos = [received] + [around(received, s) for s in range(1, narrow_count)]

    route_rows = routes.T.reshape(-1)
    hits = (route_rows[:, None] == jnp.arange(experts, dtype=I32)[None, :]).astype(BF16)
    pair_ids = jnp.arange(2 * rows, dtype=I32)
    earlier = (pair_ids[None, :] < pair_ids[:, None]).astype(BF16)
    ahead = jnp.dot(earlier, hits, preferred_element_type=F32)
    position = jnp.sum(ahead * hits.astype(F32), axis=1).astype(I32)
    slot_row = (route_rows * capacity + position).reshape(2, rows)
    slot_col = slot_row.T

    near_totals, dest = call(
        near_kernel,
        (array((tiles, TILE, 2 * width), F32), array((rows, 2 * width), F32)),
        (keys, near_count, key_col, key_row, *parts, halos[0], source_weight, dest_weight),
        scratch=(
            pltpu.VMEM((near_rows + WINDOW, 2 * width), BF16),
            pltpu.VMEM((tiles, 2 * TILE, width), BF16),
            pltpu.VMEM((CHUNK, 2 * width), F32),
            pltpu.VMEM((CHUNK, 2 * width), F32),
        ),
        smem=(0, 1),
        cost=14,
    )
    halos, near_totals, expert_in, expert_out = hold((halos, near_totals, expert_in, expert_out))
    for s in range(1, narrow_count):
        if s not in EARLY_IN:
            in_blocks[s] = around(weight_to(expert_in, s), s)
        out_blocks[s] = around(weight_to(expert_out, s), s)
    graph_out, weight_first, send = call(
        far_kernel,
        (
            array((rows, width), BF16),
            array((rows, 1), F32),
            array((experts, PANELS * capacity, 128), BF16),
        ),
        (
            keys,
            near_count,
            key_col,
            key_row,
            *halos[1:],
            source_weight,
            near_totals,
            dest,
            node_feats,
            norm_gain.reshape(1, width),
            router_weight,
            routes,
            slot_row,
            cotangent,
        ),
        scratch=(
            pltpu.VMEM((3 * per_narrow + WINDOW, 2 * width), BF16),
            pltpu.VMEM((tiles, 2 * TILE, width), BF16),
            pltpu.VMEM((CHUNK, 2 * width), F32),
            pltpu.VMEM((CHUNK, 2 * width), F32),
            pltpu.VMEM((tiles, TILE, 2 * width), F32),
        ),
        smem=(0, 1),
        cost=18,
    )
    sooner = [in_blocks[s] for s in SOON_IN] + [out_blocks[s] for s in SOON_OUT]
    send, sooner = hold((send, sooner))
    for s, block in zip(SOON_IN, sooner):
        in_blocks[s] = block
    for s, block in zip(SOON_OUT, sooner[len(SOON_IN) :]):
        out_blocks[s] = block
    arrived = lax.all_to_all(send, OWNERS, split_axis=0, concat_axis=0, tiled=True)
    blocks = in_blocks + out_blocks
    hidden_block = expert_in.shape[2]
    expert = (lax.axis_index("wide") * 2 + my_lo).astype(I32).reshape(1)
    saved = pltpu.VMEM((4, experts * capacity, hidden_block), BF16)
    packed = array((experts, 5 * capacity, 128), BF16)
    back_y = call(
        forward_kernel,
        packed,
        (expert, arrived, *blocks),
        scratch=(pltpu.VMEM((experts, width), F32),),
        smem=(0,),
        cost=8,
    )
    grad_shapes = [array((width, hidden_block), BF16)] * 4 + [array((hidden_block, width), BF16)] * 4
    grad_shapes[2] = grad_shapes[6] = array((8, 128), BF16)
    grad_shapes.append(array((2 * width * hidden_block // 128, 128), BF16))
    back_dx, *grad_blocks = call(
        backward_kernel, (packed, *grad_shapes), (arrived, *blocks), scratch=(saved, saved), cost=12
    )

    arrivals = [around(grad_blocks[i], -s) for i, s in ((1, 1), (3, 3), (5, 1), (7, 3), (8, 2))]

    def swap(back):
        return lax.all_to_all(back, OWNERS, split_axis=0, concat_axis=0, tiled=True)

    at = 4 * capacity
    back_y = swap(back_y)
    pieces = back_y[:, at : at + 8].astype(F32).reshape(experts, 2, 4, 128)
    piece = jnp.sum(pieces, axis=(0, 1))
    high = piece.astype(BF16)
    low = (piece - high.astype(F32)).astype(BF16)
    panel = jnp.concatenate([high, low, jnp.zeros((capacity - 8, 128), BF16)], axis=0)
    back_dx = lax.dynamic_update_slice(
        back_dx, jnp.broadcast_to(panel[None], (experts, capacity, 128)), (0, at, 0)
    )
    back_dx = swap(back_dx)
    layer_out, gap_grad = call(
        output_kernel,
        (array((rows, width), BF16), array((rows, 1), F32)),
        (back_y, slot_col, graph_out, weight_first, cotangent),
        cost=3,
    )
    sums = back_dx[:, at : at + 8].astype(F32).reshape(experts, 2, width)
    sums = sums[:, 0] + sums[:, 1]
    router_total = sums + lax.ppermute(sums, "hi", [(0, 1), (1, 0)])
    grad_features = call(
        input_kernel,
        array((rows, width), F32),
        (back_dx, slot_col, gap_grad, weight_first, cotangent, routes, router_weight.T),
        cost=2,
    )
    grad_features, arrivals = hold((grad_features, arrivals))
    grad_expert_in, grad_expert_out = call(
        home_kernel,
        (array(expert_in.shape, F32), array(expert_out.shape, F32)),
        (my_lo.astype(I32).reshape(1), grad_blocks[0], grad_blocks[4], *arrivals),
        smem=(0,),
        cost=2,
    )
    grad_router = router_total.T
    return (layer_out, grad_features, grad_expert_in, grad_expert_out, grad_router)


def solution(mesh):
    wide_count, narrow_count = mesh.devices.shape
    fine = Mesh(mesh.devices.reshape(wide_count, narrow_count // 2, 2), ALL)
    placed = (
        P(ALL, None),
        P("wide", NARROW, None, None),
        P(ALL, None),
        P(ALL, None),
        P(),
        P(),
        P(),
        P(),
        P(ALL, None),
        P("wide", None, NARROW),
        P("wide", NARROW, None),
        P(ALL, None),
    )
    return jax.shard_map(
        on_device,
        mesh=fine,
        in_specs=placed,
        out_specs=(
            P(ALL, None),
            P(ALL, None),
            P("wide", None, NARROW),
            P("wide", NARROW, None),
            P(),
        ),
        check_vma=False,
    )
```

```python
import jax
import jax.numpy as jnp
from jax import lax
from jax.experimental import pallas as pl
from jax.experimental.pallas import tpu as pltpu
from jax.sharding import Mesh
from jax.sharding import PartitionSpec as P

TILE = 128
CHUNK = 256
WINDOW = 512
ROW_BLOCK = 512
PANELS = 9
ALL = ("wide", "hi", "lo")
NARROW = ("hi", "lo")
OWNERS = ("wide", "lo")
F32 = jnp.float32
BF16 = jnp.bfloat16
I32 = jnp.int32
EARLY_IN = (1, 3)
SOON_IN = (2,)
SOON_OUT = (1, 3)
FLOPS_PER_US = 10**9
BYTES_PER_US = 3 * 10**6
VMEM_LIMIT = 52 * 1024 * 1024


def mm(a, b, over=((1,), (0,))):
    return lax.dot_general(a, b, (over, ((), ())), preferred_element_type=F32)


def lanes(shape):
    return lax.broadcasted_iota(I32, shape, len(shape) - 1)


def sublanes(shape):
    return lax.broadcasted_iota(I32, shape, len(shape) - 2)


def one_hot(hit):
    return jnp.where(hit, 1.0, 0.0).astype(BF16)


def call(kernel, outs, args, scratch=(), smem=(), cost=1):
    in_specs = [
        pl.BlockSpec(memory_space=pltpu.SMEM if i in smem else pltpu.VMEM) for i in range(len(args))
    ]
    return pl.pallas_call(
        kernel,
        out_shape=outs,
        in_specs=in_specs,
        out_specs=jax.tree.map(lambda _: pl.BlockSpec(memory_space=pltpu.VMEM), outs),
        scratch_shapes=list(scratch),
        compiler_params=pltpu.CompilerParams(vmem_limit_bytes=VMEM_LIMIT),
        cost_estimate=pl.CostEstimate(
            flops=cost * FLOPS_PER_US, transcendentals=0, bytes_accessed=cost * BYTES_PER_US
        ),
    )(*args)


def array(shape, dtype):
    return jax.ShapeDtypeStruct(shape, dtype)


def project(table, parts, weight):
    at = 0
    for part in parts:
        for start in range(0, part.shape[0], CHUNK):
            rows = mm(part[start : start + CHUNK], weight[...])
            table[at : at + CHUNK] = rows.astype(BF16)
            at += CHUNK
    table[at:] = jnp.zeros((WINDOW, table.shape[1]), BF16)


def split_dest(dest, dest_parts):
    high = dest.astype(BF16)
    low = (dest - high.astype(F32)).astype(BF16)
    for t in range(dest_parts.shape[0]):
        dest_parts[t, :TILE] = high[t * TILE : (t + 1) * TILE]
        dest_parts[t, TILE:] = low[t * TILE : (t + 1) * TILE]


def add_edges(chunks, base, limit, keys, key_col, key_row, table, dest_parts, picked, totals):
    width = dest_parts.shape[2]
    spot = lanes((CHUNK, WINDOW))
    tile_spot = lanes((CHUNK, 2 * TILE)) & (TILE - 1)

    def gather(t, c, k):
        first = jnp.clip((keys[t, c * CHUNK] >> 8) - base, 0, limit - base) & ~15
        at = pl.multiple_of(first + k * WINDOW, 16)
        key = key_col[t, pl.ds(pl.multiple_of(c * CHUNK, CHUNK), CHUNK), :]
        row = (key >> 8) - (base + at)
        return mm(one_hot(row == spot), table[pl.ds(at, WINDOW), :])

    def more(t, c):
        first = jnp.clip((keys[t, c * CHUNK] >> 8) - base, 0, limit - base) & ~15
        last = jnp.minimum(keys[t, c * CHUNK + CHUNK - 1] >> 8, limit - 1) - base

        def window(k, carry):
            picked[t][...] += gather(t, c, k)
            return carry

        lax.fori_loop(1, (jnp.maximum(last - first, 0) >> 9) + 1, window, 0)

    def add(t, c, live):
        start = pl.multiple_of(c * CHUNK, CHUNK)
        key = key_col[t, pl.ds(start, CHUNK), :]
        dest_gate = mm(one_hot((key & 255) == tile_spot), dest_parts[t])
        pre = picked[t][:, :width] + dest_gate
        gates = (0.5 * jnp.tanh(0.5 * pre) + 0.5).astype(BF16)
        messages = gates * picked[t][:, width:].astype(BF16)
        row_key = key_row[t, :, pl.ds(start, CHUNK)]
        source = row_key >> 8
        target = jnp.where((source >= base) & (source < limit) & live, row_key & 255, 255)
        selector = one_hot(target == sublanes((TILE, CHUNK)))
        totals[t, :, :width] += mm(selector, messages)
        totals[t, :, width:] += mm(selector, gates)

    picked[1][...] = jnp.zeros_like(picked[1])
    begin, end = chunks

    def both(c, carry):
        picked[0][...] = gather(0, c, 0)
        add(1, jnp.maximum(c - 1, 0), c > begin)
        more(0, c)
        picked[1][...] = gather(1, c, 0)
        add(0, c, c >= begin)
        more(1, c)
        return carry

    lax.fori_loop(begin, end, both, 0)
    add(1, jnp.maximum(end - 1, 0), end > begin)


def near_kernel(
    keys,
    near_count,
    key_col,
    key_row,
    own,
    back_one,
    back_two,
    back_three,
    halo,
    source_weight,
    dest_weight,
    totals,
    dest,
    table,
    dest_parts,
    picked_one,
    picked_two,
):
    rows, width = own.shape
    project(table, (own, back_one, back_two, back_three, halo), source_weight)
    dest[...] = mm(own[...], dest_weight[...])
    split_dest(dest[:, :width], dest_parts)
    totals[...] = jnp.zeros_like(totals)
    limit = 4 * rows + halo.shape[0]
    chunks = (0, (jnp.maximum(near_count[0], near_count[1]) + CHUNK - 1) // CHUNK)
    picked = (picked_one, picked_two)
    add_edges(chunks, 0, limit, keys, key_col, key_row, table, dest_parts, picked, totals)


def far_kernel(
    keys,
    near_count,
    key_col,
    key_row,
    halo_one,
    halo_two,
    halo_three,
    source_weight,
    near_totals,
    dest,
    own,
    norm_gain,
    router_weight,
    routes,
    slot_row,
    cotangent,
    graph_out,
    weight_first,
    send,
    table,
    dest_parts,
    picked_one,
    picked_two,
    totals,
):
    rows, width = own.shape
    project(table, (halo_one, halo_two, halo_three), source_weight)
    split_dest(dest[:, :width], dest_parts)
    totals[...] = near_totals[...]
    base = 4 * rows + halo_one.shape[0]
    limit = base + 3 * halo_one.shape[0]
    chunks = (jnp.minimum(near_count[0], near_count[1]) // CHUNK, keys.shape[1] // CHUNK)
    picked = (picked_one, picked_two)
    add_edges(chunks, base, limit, keys, key_col, key_row, table, dest_parts, picked, totals)

    whole = totals[...].reshape(rows, 2 * width)
    agg = whole[:, :width] / jnp.maximum(whole[:, width:], 1.0)
    pre_norm = dest[:, width:] + agg
    average = jnp.mean(pre_norm, axis=1, keepdims=True)
    center = pre_norm - average
    variance = jnp.mean(center * center, axis=1, keepdims=True)
    normed = center * lax.rsqrt(variance + 1e-05) * norm_gain[...]
    result = (own[...].astype(F32) + jnp.maximum(normed, 0.0)).astype(BF16)
    graph_out[...] = result

    logits = mm(result, router_weight[...])
    gap_mask = hit_gap(routes, logits.shape)
    first_weight = jax.nn.sigmoid(jnp.sum(logits * gap_mask, axis=1, keepdims=True))
    weight_first[...] = first_weight
    cot = cotangent[...].astype(F32)
    grads_first = (first_weight * cot).astype(BF16)
    grads_second = ((1.0 - first_weight) * cot).astype(BF16)
    experts = router_weight.shape[1]
    capacity = send.shape[1] // PANELS
    slot = sublanes((experts * capacity, rows))
    to_first = one_hot(slot_row[0:1, :] == slot)
    to_second = one_hot(slot_row[1:2, :] == slot)
    rows_out = mm(to_first + to_second, result).astype(BF16)
    grads_out = (mm(to_first, grads_first) + mm(to_second, grads_second)).astype(BF16)
    about_first = about(1.0 - first_weight, routes[:, 1:2])
    about_second = about(first_weight, routes[:, 0:1])
    about_out = (mm(to_first, about_first) + mm(to_second, about_second)).astype(BF16)
    panels = [v[:, i : i + 128] for v in (rows_out, grads_out) for i in range(0, width, 128)]
    for p, panel in enumerate(panels + [about_out]):
        send[:, p * capacity : (p + 1) * capacity] = panel.reshape(experts, capacity, 128)


def about(weight, expert):
    high = weight.astype(BF16).astype(F32)
    lane = lanes((weight.shape[0], 128))
    parts = jnp.where(lane == 0, high, jnp.where(lane == 1, weight - high, 0.0))
    return jnp.where(lane == 2, expert.astype(F32), parts).astype(BF16)


def hit_gap(routes, shape):
    spot = lanes(shape)
    first = jnp.where(routes[:, 0:1] == spot, 1.0, 0.0)
    second = jnp.where(routes[:, 1:2] == spot, 1.0, 0.0)
    return first - second


def unpack(arrived, chunks, capacity, start, count):
    parts = [
        arrived[chunks, p * capacity : (p + 1) * capacity].reshape(-1, 128)
        for p in range(start, start + count)
    ]
    return jnp.concatenate(parts, axis=1)


def expert_kernel(expert, arrived, *refs):
    ins, outs = refs[:4], refs[4:8]
    back, router_part, act_all, hidden_all, router_sum = refs[8:]
    chunk_count = arrived.shape[0]
    _, _, capacity, width = back.shape
    step = ROW_BLOCK // capacity
    experts = router_part.shape[0]
    router_sum[...] = jnp.zeros_like(router_sum)

    def block(b, carry):
        at = pl.ds(pl.multiple_of(b * ROW_BLOCK, ROW_BLOCK), ROW_BLOCK)
        chunks = pl.ds(b * step, step)
        rows = unpack(arrived, chunks, capacity, 0, 4)
        grads = unpack(arrived, chunks, capacity, 4, 4)
        other = unpack(arrived, chunks, capacity, 8, 1).astype(F32)
        y, dx = None, None
        for s, (w_in, w_out) in enumerate(zip(ins, outs)):
            x = mm(rows, w_in[...])
            square = x * x
            tanh = jnp.tanh(x * (0.7978845608028654 + 0.035677408136300125 * square))
            half = 0.5 + 0.5 * tanh
            active = (x * half).astype(BF16)
            slope = 0.7978845608028654 + 0.10703222440890037 * square
            back_slope = half + 0.5 * x * (1.0 - tanh * tanh) * slope
            hidden = (back_slope * mm(grads, w_out[...], ((1,), (1,)))).astype(BF16)
            act_all[s, at, :] = active
            hidden_all[s, at, :] = hidden
            y_part = mm(active, w_out[...])
            dx_part = mm(hidden, w_in[...], ((1,), (1,)))
            y = y_part if y is None else y + y_part
            dx = dx_part if dx is None else dx + dx_part
        back[chunks, 0] = y.astype(BF16).reshape(step, capacity, width)
        back[chunks, 1] = dx.astype(BF16).reshape(step, capacity, width)
        share = jnp.sum(grads.astype(F32) * y, axis=1, keepdims=True)
        share = share * (other[:, 0:1] + other[:, 1:2])
        lane = lanes((ROW_BLOCK, experts))
        own_lane = jnp.where(lane == expert[0], 1.0, 0.0)
        other_lane = jnp.where(lane.astype(F32) == other[:, 2:3], 1.0, 0.0)
        shares = share * (own_lane - other_lane)
        high = shares.astype(BF16)
        low = (shares - high.astype(F32)).astype(BF16)
        both = mm(jnp.concatenate([high, low], axis=1), rows, ((0,), (0,)))
        router_sum[...] += both[:experts] + both[experts:]
        return carry

    lax.fori_loop(0, chunk_count // step, block, 0)
    router_part[...] = router_sum[...]


def weight_kernel(arrived, act_all, hidden_all, *blocks):
    capacity = arrived.shape[1] // PANELS
    rows = unpack(arrived, slice(None), capacity, 0, 4)
    grads = unpack(arrived, slice(None), capacity, 4, 4)
    for s in range(4):
        blocks[s][...] = mm(rows, hidden_all[s], ((0,), (0,))).astype(BF16)
        blocks[4 + s][...] = mm(act_all[s], grads, ((0,), (0,))).astype(BF16)


def output_kernel(
    back,
    slot_col,
    graph_out,
    weight_first,
    cotangent,
    routes,
    router_t,
    layer_out,
    grad_features,
):
    rows, width = graph_out.shape
    slot = lanes((rows, slot_col.shape[1] // 2 * back.shape[0] * back.shape[2]))
    to_first = one_hot(slot_col[:, 0:1] == slot)
    to_second = one_hot(slot_col[:, 1:2] == slot)
    one, two = weight_first[...], 1.0 - weight_first[...]
    y = back[:, 0].reshape(-1, width)
    first, second = mm(to_first, y), mm(to_second, y)
    layer_out[...] = (graph_out[...].astype(F32) + (one * first + two * second)).astype(BF16)
    cot = cotangent[...].astype(F32)
    gap = jnp.sum(cot * (first - second), axis=1, keepdims=True) * one * two
    dx = back[:, 1].reshape(-1, width)
    mixed = one * mm(to_first, dx) + two * mm(to_second, dx)
    spread = mm(hit_gap(routes, (rows, router_t.shape[0])).astype(BF16), router_t[...])
    grad_features[...] = cot + mixed + gap * spread


def halo_kernel(list_col, node_feats, send):
    pick = one_hot(list_col[...] == lanes((list_col.shape[0], node_feats.shape[0])))
    send[...] = mm(pick, node_feats[...]).astype(BF16).reshape(send.shape)


def hold(values):
    return lax.optimization_barrier(values)


def ring(n, s):
    return [(i, (i + s) % n) for i in range(n)]


def along(wide_count, unit, shift):
    def to(i):
        return i - (i // unit % 4) * unit + ((i // unit + shift) % 4) * unit

    return [(i, to(i)) for i in range(wide_count)]


def add_axis(value, names, pairs):
    sent = value.astype(BF16)
    one, two, three = (lax.ppermute(sent, names, pairs(s)).astype(F32) for s in (1, 2, 3))
    return (sent.astype(F32) + two) + (one + three)


def on_device(
    node_feats,
    halo_rows,
    edge_src,
    edge_dst,
    dest_weight,
    source_weight,
    norm_gain,
    router_weight,
    routes,
    expert_in,
    expert_out,
    cotangent,
):
    rows, width = node_feats.shape
    wide_count = lax.axis_size("wide")
    narrow_count = lax.axis_size("hi") * lax.axis_size("lo")
    my_lo = lax.axis_index("lo")
    me = lax.axis_index("hi") * 2 + my_lo
    peer = halo_rows.shape[-1]
    part_rows = narrow_count * rows
    experts = router_weight.shape[1]
    capacity = 4 * rows // experts
    tiles, slots = edge_src.shape

    def around(value, s):
        return lax.ppermute(value, NARROW, ring(narrow_count, s))

    def weight_to(weight, s):
        which = (my_lo + s) % 2
        return lax.dynamic_index_in_dim(weight, which, 0, keepdims=False)

    in_blocks = [weight_to(expert_in, 0)] + [None] * 3
    out_blocks = [weight_to(expert_out, 0)] + [None] * 3

    per_narrow = wide_count * peer
    local = edge_src < part_rows
    halo_id = edge_src - part_rows
    size = jnp.where(local, rows, per_narrow)
    offset = jnp.where(local, edge_src, halo_id)
    place = (me - offset // size) % narrow_count * size + offset % size
    place = place + jnp.where(local, 0, part_rows)
    keys = lax.sort(place * 256 + edge_dst, dimension=1)
    near_rows = part_rows + per_narrow
    near_count = jnp.sum((keys < near_rows * 256).astype(I32), axis=1)
    key_col = keys.reshape(tiles, slots, 1)
    key_row = keys.reshape(tiles, 1, slots)

    halo_send = call(
        halo_kernel,
        array((wide_count, peer, width), BF16),
        (halo_rows.reshape(-1, 1), node_feats),
    )
    received = lax.all_to_all(halo_send, "wide", split_axis=0, concat_axis=0, tiled=True)
    received = received.reshape(-1, width)
    parts = [node_feats] + [around(node_feats, s) for s in range(1, narrow_count)]
    for s in EARLY_IN:
        in_blocks[s] = around(weight_to(expert_in, s), s)
    received, parts, in_blocks, keys, key_col, key_row, near_count = hold(
        (received, parts, in_blocks, keys, key_col, key_row, near_count)
    )
    halos = [received] + [around(received, s) for s in range(1, narrow_count)]

    route_rows = routes.T.reshape(-1)
    hits = (route_rows[:, None] == jnp.arange(experts, dtype=I32)[None, :]).astype(BF16)
    pair_ids = jnp.arange(2 * rows, dtype=I32)
    earlier = (pair_ids[None, :] < pair_ids[:, None]).astype(BF16)
    ahead = jnp.dot(earlier, hits, preferred_element_type=F32)
    position = jnp.sum(ahead * hits.astype(F32), axis=1).astype(I32)
    slot_row = (route_rows * capacity + position).reshape(2, rows)
    slot_col = slot_row.T

    near_totals, dest = call(
        near_kernel,
        (array((tiles, TILE, 2 * width), F32), array((rows, 2 * width), F32)),
        (keys, near_count, key_col, key_row, *parts, halos[0], source_weight, dest_weight),
        scratch=(
            pltpu.VMEM((near_rows + WINDOW, 2 * width), BF16),
            pltpu.VMEM((tiles, 2 * TILE, width), BF16),
            pltpu.VMEM((CHUNK, 2 * width), F32),
            pltpu.VMEM((CHUNK, 2 * width), F32),
        ),
        smem=(0, 1),
        cost=14,
    )
    halos, near_totals, expert_in, expert_out = hold((halos, near_totals, expert_in, expert_out))
    for s in range(1, narrow_count):
        if s not in EARLY_IN:
            in_blocks[s] = around(weight_to(expert_in, s), s)
        out_blocks[s] = around(weight_to(expert_out, s), s)
    graph_out, weight_first, send = call(
        far_kernel,
        (
            array((rows, width), BF16),
            array((rows, 1), F32),
            array((experts, PANELS * capacity, 128), BF16),
        ),
        (
            keys,
            near_count,
            key_col,
            key_row,
            *halos[1:],
            source_weight,
            near_totals,
            dest,
            node_feats,
            norm_gain.reshape(1, width),
            router_weight,
            routes,
            slot_row,
            cotangent,
        ),
        scratch=(
            pltpu.VMEM((3 * per_narrow + WINDOW, 2 * width), BF16),
            pltpu.VMEM((tiles, 2 * TILE, width), BF16),
            pltpu.VMEM((CHUNK, 2 * width), F32),
            pltpu.VMEM((CHUNK, 2 * width), F32),
            pltpu.VMEM((tiles, TILE, 2 * width), F32),
        ),
        smem=(0, 1),
        cost=18,
    )
    sooner = [in_blocks[s] for s in SOON_IN] + [out_blocks[s] for s in SOON_OUT]
    send, sooner = hold((send, sooner))
    for s, block in zip(SOON_IN, sooner):
        in_blocks[s] = block
    for s, block in zip(SOON_OUT, sooner[len(SOON_IN) :]):
        out_blocks[s] = block
    arrived = lax.all_to_all(send, OWNERS, split_axis=0, concat_axis=0, tiled=True)
    blocks = in_blocks + out_blocks
    hidden_block = expert_in.shape[2]
    expert = (lax.axis_index("wide") * 2 + my_lo).astype(I32).reshape(1)
    saved = array((4, experts * capacity, hidden_block), BF16)
    back, router_part, act_all, hidden_all = call(
        expert_kernel,
        (
            array((experts, 2, capacity, width), BF16),
            array((experts, width), F32),
            saved,
            saved,
        ),
        (expert, arrived, *blocks),
        scratch=(pltpu.VMEM((experts, width), F32),),
        smem=(0,),
        cost=12,
    )
    router_part = router_part.astype(BF16)
    twin = lax.ppermute(router_part, "wide", [(i, i ^ 1) for i in range(wide_count)])
    router_sum = router_part.astype(F32) + twin.astype(F32)
    back = lax.all_to_all(
        back.reshape(experts, 2 * capacity, width), OWNERS, split_axis=0, concat_axis=0, tiled=True
    ).reshape(experts, 2, capacity, width)
    grad_shapes = [array((width, hidden_block), BF16)] * 4 + [array((hidden_block, width), BF16)] * 4
    grad_blocks = call(weight_kernel, grad_shapes, (arrived, act_all, hidden_all), cost=5)

    def sent_home(grads):
        return [grads[0]] + [around(grads[s], -s) for s in range(1, narrow_count)]

    def home(back):
        mine = back[0].astype(F32) + back[2].astype(F32)
        other = back[1].astype(F32) + back[3].astype(F32)
        low = my_lo == 0
        return jnp.stack([jnp.where(low, mine, other), jnp.where(low, other, mine)])

    in_back = sent_home(grad_blocks[:4])
    out_back = sent_home(grad_blocks[4:])
    router_sum = add_axis(router_sum, NARROW, lambda s: ring(narrow_count, s))
    router_sum, back, in_back = hold((router_sum, back, in_back))
    router_sum = add_axis(router_sum, "wide", lambda s: along(wide_count, 2, s))
    router_sum, out_back = hold((router_sum, out_back))
    router_total = add_axis(router_sum, "wide", lambda s: along(wide_count, 8, s))
    layer_out, grad_features = call(
        output_kernel,
        (array((rows, width), BF16), array((rows, width), F32)),
        (back, slot_col, graph_out, weight_first, cotangent, routes, router_weight.T),
        cost=5,
    )
    grad_expert_in = home(in_back)
    grad_expert_out = home(out_back)
    grad_router = router_total.T
    return (layer_out, grad_features, grad_expert_in, grad_expert_out, grad_router)


def solution(mesh):
    wide_count, narrow_count = mesh.devices.shape
    fine = Mesh(mesh.devices.reshape(wide_count, narrow_count // 2, 2), ALL)
    placed = (
        P(ALL, None),
        P("wide", NARROW, None, None),
        P(ALL, None),
        P(ALL, None),
        P(),
        P(),
        P(),
        P(),
        P(ALL, None),
        P("wide", None, NARROW),
        P("wide", NARROW, None),
        P(ALL, None),
    )
    return jax.shard_map(
        on_device,
        mesh=fine,
        in_specs=placed,
        out_specs=(
            P(ALL, None),
            P(ALL, None),
            P("wide", None, NARROW),
            P("wide", NARROW, None),
            P(),
        ),
        check_vma=False,
    )
```

```python
import jax
import jax.numpy as jnp
from jax import lax
from jax.experimental import pallas as pl
from jax.experimental.pallas import tpu as pltpu
from jax.sharding import Mesh
from jax.sharding import PartitionSpec as P

TILE = 128
CHUNK = 256
WINDOW = 512
ROW_BLOCK = 512
PANELS = 9
ALL = ("wide", "hi", "lo")
NARROW = ("hi", "lo")
OWNERS = ("wide", "lo")
F32 = jnp.float32
BF16 = jnp.bfloat16
I32 = jnp.int32
EARLY_IN = (1, 3)
SOON_IN = (2,)
SOON_OUT = (1, 3)
FLOPS_PER_US = 10**9
BYTES_PER_US = 3 * 10**6
VMEM_LIMIT = 52 * 1024 * 1024


def mm(a, b, over=((1,), (0,))):
    return lax.dot_general(a, b, (over, ((), ())), preferred_element_type=F32)


def lanes(shape):
    return lax.broadcasted_iota(I32, shape, len(shape) - 1)


def sublanes(shape):
    return lax.broadcasted_iota(I32, shape, len(shape) - 2)


def one_hot(hit):
    return jnp.where(hit, 1.0, 0.0).astype(BF16)


def call(kernel, outs, args, scratch=(), smem=(), cost=1):
    in_specs = [
        pl.BlockSpec(memory_space=pltpu.SMEM if i in smem else pltpu.VMEM) for i in range(len(args))
    ]
    return pl.pallas_call(
        kernel,
        out_shape=outs,
        in_specs=in_specs,
        out_specs=jax.tree.map(lambda _: pl.BlockSpec(memory_space=pltpu.VMEM), outs),
        scratch_shapes=list(scratch),
        compiler_params=pltpu.CompilerParams(vmem_limit_bytes=VMEM_LIMIT),
        cost_estimate=pl.CostEstimate(
            flops=cost * FLOPS_PER_US, transcendentals=0, bytes_accessed=cost * BYTES_PER_US
        ),
    )(*args)


def array(shape, dtype):
    return jax.ShapeDtypeStruct(shape, dtype)


def project(table, parts, weight):
    at = 0
    for part in parts:
        for start in range(0, part.shape[0], CHUNK):
            rows = mm(part[start : start + CHUNK], weight[...])
            table[at : at + CHUNK] = rows.astype(BF16)
            at += CHUNK
    table[at:] = jnp.zeros((WINDOW, table.shape[1]), BF16)


def split_dest(dest, dest_parts):
    high = dest.astype(BF16)
    low = (dest - high.astype(F32)).astype(BF16)
    for t in range(dest_parts.shape[0]):
        dest_parts[t, :TILE] = high[t * TILE : (t + 1) * TILE]
        dest_parts[t, TILE:] = low[t * TILE : (t + 1) * TILE]


def add_edges(chunks, base, limit, keys, key_col, key_row, table, dest_parts, picked, totals):
    width = dest_parts.shape[2]
    spot = lanes((CHUNK, WINDOW))
    tile_spot = lanes((CHUNK, 2 * TILE)) & (TILE - 1)

    def gather(t, c, k):
        first = jnp.clip((keys[t, c * CHUNK] >> 8) - base, 0, limit - base) & ~15
        at = pl.multiple_of(first + k * WINDOW, 16)
        key = key_col[t, pl.ds(pl.multiple_of(c * CHUNK, CHUNK), CHUNK), :]
        row = (key >> 8) - (base + at)
        return mm(one_hot(row == spot), table[pl.ds(at, WINDOW), :])

    def more(t, c):
        first = jnp.clip((keys[t, c * CHUNK] >> 8) - base, 0, limit - base) & ~15
        last = jnp.minimum(keys[t, c * CHUNK + CHUNK - 1] >> 8, limit - 1) - base

        def window(k, carry):
            picked[t][...] += gather(t, c, k)
            return carry

        lax.fori_loop(1, (jnp.maximum(last - first, 0) >> 9) + 1, window, 0)

    def add(t, c, live):
        start = pl.multiple_of(c * CHUNK, CHUNK)
        key = key_col[t, pl.ds(start, CHUNK), :]
        dest_gate = mm(one_hot((key & 255) == tile_spot), dest_parts[t])
        pre = picked[t][:, :width] + dest_gate
        gates = (0.5 * jnp.tanh(0.5 * pre) + 0.5).astype(BF16)
        messages = gates * picked[t][:, width:].astype(BF16)
        row_key = key_row[t, :, pl.ds(start, CHUNK)]
        source = row_key >> 8
        target = jnp.where((source >= base) & (source < limit) & live, row_key & 255, 255)
        selector = one_hot(target == sublanes((TILE, CHUNK)))
        totals[t, :, :width] += mm(selector, messages)
        totals[t, :, width:] += mm(selector, gates)

    picked[1][...] = jnp.zeros_like(picked[1])
    begin, end = chunks

    def both(c, carry):
        picked[0][...] = gather(0, c, 0)
        add(1, jnp.maximum(c - 1, 0), c > begin)
        more(0, c)
        picked[1][...] = gather(1, c, 0)
        add(0, c, c >= begin)
        more(1, c)
        return carry

    lax.fori_loop(begin, end, both, 0)
    add(1, jnp.maximum(end - 1, 0), end > begin)


def near_kernel(
    keys,
    near_count,
    key_col,
    key_row,
    own,
    back_one,
    back_two,
    back_three,
    halo,
    source_weight,
    dest_weight,
    totals,
    dest,
    table,
    dest_parts,
    picked_one,
    picked_two,
):
    rows, width = own.shape
    project(table, (own, back_one, back_two, back_three, halo), source_weight)
    dest[...] = mm(own[...], dest_weight[...])
    split_dest(dest[:, :width], dest_parts)
    totals[...] = jnp.zeros_like(totals)
    limit = 4 * rows + halo.shape[0]
    chunks = (0, (jnp.maximum(near_count[0], near_count[1]) + CHUNK - 1) // CHUNK)
    picked = (picked_one, picked_two)
    add_edges(chunks, 0, limit, keys, key_col, key_row, table, dest_parts, picked, totals)


def far_kernel(
    keys,
    near_count,
    key_col,
    key_row,
    halo_one,
    halo_two,
    halo_three,
    source_weight,
    near_totals,
    dest,
    own,
    norm_gain,
    router_weight,
    routes,
    slot_row,
    cotangent,
    graph_out,
    weight_first,
    send,
    table,
    dest_parts,
    picked_one,
    picked_two,
    totals,
):
    rows, width = own.shape
    project(table, (halo_one, halo_two, halo_three), source_weight)
    split_dest(dest[:, :width], dest_parts)
    totals[...] = near_totals[...]
    base = 4 * rows + halo_one.shape[0]
    limit = base + 3 * halo_one.shape[0]
    chunks = (jnp.minimum(near_count[0], near_count[1]) // CHUNK, keys.shape[1] // CHUNK)
    picked = (picked_one, picked_two)
    add_edges(chunks, base, limit, keys, key_col, key_row, table, dest_parts, picked, totals)

    whole = totals[...].reshape(rows, 2 * width)
    agg = whole[:, :width] / jnp.maximum(whole[:, width:], 1.0)
    pre_norm = dest[:, width:] + agg
    average = jnp.mean(pre_norm, axis=1, keepdims=True)
    center = pre_norm - average
    variance = jnp.mean(center * center, axis=1, keepdims=True)
    normed = center * lax.rsqrt(variance + 1e-05) * norm_gain[...]
    result = (own[...].astype(F32) + jnp.maximum(normed, 0.0)).astype(BF16)
    graph_out[...] = result

    logits = mm(result, router_weight[...])
    gap_mask = hit_gap(routes, logits.shape)
    first_weight = jax.nn.sigmoid(jnp.sum(logits * gap_mask, axis=1, keepdims=True))
    weight_first[...] = first_weight
    cot = cotangent[...].astype(F32)
    grads_first = (first_weight * cot).astype(BF16)
    grads_second = ((1.0 - first_weight) * cot).astype(BF16)
    experts = router_weight.shape[1]
    capacity = send.shape[1] // PANELS
    slot = sublanes((experts * capacity, rows))
    to_first = one_hot(slot_row[0:1, :] == slot)
    to_second = one_hot(slot_row[1:2, :] == slot)
    rows_out = mm(to_first + to_second, result).astype(BF16)
    grads_out = (mm(to_first, grads_first) + mm(to_second, grads_second)).astype(BF16)
    about_first = about(1.0 - first_weight, routes[:, 1:2])
    about_second = about(first_weight, routes[:, 0:1])
    about_out = (mm(to_first, about_first) + mm(to_second, about_second)).astype(BF16)
    panels = [v[:, i : i + 128] for v in (rows_out, grads_out) for i in range(0, width, 128)]
    for p, panel in enumerate(panels + [about_out]):
        send[:, p * capacity : (p + 1) * capacity] = panel.reshape(experts, capacity, 128)


def about(weight, expert):
    high = weight.astype(BF16).astype(F32)
    lane = lanes((weight.shape[0], 128))
    parts = jnp.where(lane == 0, high, jnp.where(lane == 1, weight - high, 0.0))
    return jnp.where(lane == 2, expert.astype(F32), parts).astype(BF16)


def hit_gap(routes, shape):
    spot = lanes(shape)
    first = jnp.where(routes[:, 0:1] == spot, 1.0, 0.0)
    second = jnp.where(routes[:, 1:2] == spot, 1.0, 0.0)
    return first - second


def unpack(arrived, chunks, capacity, start, count):
    parts = [
        arrived[chunks, p * capacity : (p + 1) * capacity].reshape(-1, 128)
        for p in range(start, start + count)
    ]
    return jnp.concatenate(parts, axis=1)


def expert_kernel(expert, arrived, *refs):
    ins, outs = refs[:4], refs[4:8]
    back, router_part, act_all, hidden_all, router_sum = refs[8:]
    chunk_count = arrived.shape[0]
    _, _, capacity, width = back.shape
    step = ROW_BLOCK // capacity
    experts = router_part.shape[0]
    router_sum[...] = jnp.zeros_like(router_sum)

    def block(b, carry):
        at = pl.ds(pl.multiple_of(b * ROW_BLOCK, ROW_BLOCK), ROW_BLOCK)
        chunks = pl.ds(b * step, step)
        rows = unpack(arrived, chunks, capacity, 0, 4)
        grads = unpack(arrived, chunks, capacity, 4, 4)
        other = unpack(arrived, chunks, capacity, 8, 1).astype(F32)
        y, dx = None, None
        for s, (w_in, w_out) in enumerate(zip(ins, outs)):
            x = mm(rows, w_in[...])
            square = x * x
            tanh = jnp.tanh(x * (0.7978845608028654 + 0.035677408136300125 * square))
            half = 0.5 + 0.5 * tanh
            active = (x * half).astype(BF16)
            slope = 0.7978845608028654 + 0.10703222440890037 * square
            back_slope = half + 0.5 * x * (1.0 - tanh * tanh) * slope
            hidden = (back_slope * mm(grads, w_out[...], ((1,), (1,)))).astype(BF16)
            act_all[s, at, :] = active
            hidden_all[s, at, :] = hidden
            y_part = mm(active, w_out[...])
            dx_part = mm(hidden, w_in[...], ((1,), (1,)))
            y = y_part if y is None else y + y_part
            dx = dx_part if dx is None else dx + dx_part
        back[chunks, 0] = y.astype(BF16).reshape(step, capacity, width)
        back[chunks, 1] = dx.astype(BF16).reshape(step, capacity, width)
        share = jnp.sum(grads.astype(F32) * y, axis=1, keepdims=True)
        share = share * (other[:, 0:1] + other[:, 1:2])
        lane = lanes((ROW_BLOCK, experts))
        own_lane = jnp.where(lane == expert[0], 1.0, 0.0)
        other_lane = jnp.where(lane.astype(F32) == other[:, 2:3], 1.0, 0.0)
        shares = share * (own_lane - other_lane)
        high = shares.astype(BF16)
        low = (shares - high.astype(F32)).astype(BF16)
        both = mm(jnp.concatenate([high, low], axis=1), rows, ((0,), (0,)))
        router_sum[...] += both[:experts] + both[experts:]
        return carry

    lax.fori_loop(0, chunk_count // step, block, 0)
    router_part[...] = router_sum[...]


def weight_kernel(arrived, act_all, hidden_all, *blocks):
    capacity = arrived.shape[1] // PANELS
    rows = unpack(arrived, slice(None), capacity, 0, 4)
    grads = unpack(arrived, slice(None), capacity, 4, 4)
    for s in range(4):
        blocks[s][...] = mm(rows, hidden_all[s], ((0,), (0,))).astype(BF16)
        blocks[4 + s][...] = mm(act_all[s], grads, ((0,), (0,))).astype(BF16)


def output_kernel(
    back,
    slot_col,
    graph_out,
    weight_first,
    cotangent,
    routes,
    router_t,
    layer_out,
    grad_features,
):
    rows, width = graph_out.shape
    slot = lanes((rows, slot_col.shape[1] // 2 * back.shape[0] * back.shape[2]))
    to_first = one_hot(slot_col[:, 0:1] == slot)
    to_second = one_hot(slot_col[:, 1:2] == slot)
    one, two = weight_first[...], 1.0 - weight_first[...]
    y = back[:, 0].reshape(-1, width)
    first, second = mm(to_first, y), mm(to_second, y)
    layer_out[...] = (graph_out[...].astype(F32) + (one * first + two * second)).astype(BF16)
    cot = cotangent[...].astype(F32)
    gap = jnp.sum(cot * (first - second), axis=1, keepdims=True) * one * two
    dx = back[:, 1].reshape(-1, width)
    mixed = one * mm(to_first, dx) + two * mm(to_second, dx)
    spread = mm(hit_gap(routes, (rows, router_t.shape[0])).astype(BF16), router_t[...])
    grad_features[...] = cot + mixed + gap * spread


def halo_kernel(list_col, node_feats, send):
    pick = one_hot(list_col[...] == lanes((list_col.shape[0], node_feats.shape[0])))
    send[...] = mm(pick, node_feats[...]).astype(BF16).reshape(send.shape)


def hold(values):
    return lax.optimization_barrier(values)


def ring(n, s):
    return [(i, (i + s) % n) for i in range(n)]


def along(wide_count, unit, shift):
    def to(i):
        return i - (i // unit % 4) * unit + ((i // unit + shift) % 4) * unit

    return [(i, to(i)) for i in range(wide_count)]


def add_axis(value, names, pairs):
    sent = value.astype(BF16)
    one, two, three = (lax.ppermute(sent, names, pairs(s)).astype(F32) for s in (1, 2, 3))
    return (sent.astype(F32) + two) + (one + three)


def on_device(
    node_feats,
    halo_rows,
    edge_src,
    edge_dst,
    dest_weight,
    source_weight,
    norm_gain,
    router_weight,
    routes,
    expert_in,
    expert_out,
    cotangent,
):
    rows, width = node_feats.shape
    wide_count = lax.axis_size("wide")
    narrow_count = lax.axis_size("hi") * lax.axis_size("lo")
    my_lo = lax.axis_index("lo")
    me = lax.axis_index("hi") * 2 + my_lo
    peer = halo_rows.shape[-1]
    part_rows = narrow_count * rows
    experts = router_weight.shape[1]
    capacity = 4 * rows // experts
    tiles, slots = edge_src.shape

    def around(value, s):
        return lax.ppermute(value, NARROW, ring(narrow_count, s))

    def weight_to(weight, s):
        which = (my_lo + s) % 2
        return lax.dynamic_index_in_dim(weight, which, 0, keepdims=False)

    in_blocks = [weight_to(expert_in, 0)] + [None] * 3
    out_blocks = [weight_to(expert_out, 0)] + [None] * 3

    per_narrow = wide_count * peer
    local = edge_src < part_rows
    halo_id = edge_src - part_rows
    size = jnp.where(local, rows, per_narrow)
    offset = jnp.where(local, edge_src, halo_id)
    place = (me - offset // size) % narrow_count * size + offset % size
    place = place + jnp.where(local, 0, part_rows)
    keys = lax.sort(place * 256 + edge_dst, dimension=1)
    near_rows = part_rows + per_narrow
    near_count = jnp.sum((keys < near_rows * 256).astype(I32), axis=1)
    key_col = keys.reshape(tiles, slots, 1)
    key_row = keys.reshape(tiles, 1, slots)

    halo_send = call(
        halo_kernel,
        array((wide_count, peer, width), BF16),
        (halo_rows.reshape(-1, 1), node_feats),
    )
    received = lax.all_to_all(halo_send, "wide", split_axis=0, concat_axis=0, tiled=True)
    received = received.reshape(-1, width)
    parts = [node_feats] + [around(node_feats, s) for s in range(1, narrow_count)]
    for s in EARLY_IN:
        in_blocks[s] = around(weight_to(expert_in, s), s)
    received, parts, in_blocks, keys, key_col, key_row, near_count = hold(
        (received, parts, in_blocks, keys, key_col, key_row, near_count)
    )
    halos = [received] + [around(received, s) for s in range(1, narrow_count)]

    route_rows = routes.T.reshape(-1)
    hits = (route_rows[:, None] == jnp.arange(experts, dtype=I32)[None, :]).astype(BF16)
    pair_ids = jnp.arange(2 * rows, dtype=I32)
    earlier = (pair_ids[None, :] < pair_ids[:, None]).astype(BF16)
    ahead = jnp.dot(earlier, hits, preferred_element_type=F32)
    position = jnp.sum(ahead * hits.astype(F32), axis=1).astype(I32)
    slot_row = (route_rows * capacity + position).reshape(2, rows)
    slot_col = slot_row.T

    near_totals, dest = call(
        near_kernel,
        (array((tiles, TILE, 2 * width), F32), array((rows, 2 * width), F32)),
        (keys, near_count, key_col, key_row, *parts, halos[0], source_weight, dest_weight),
        scratch=(
            pltpu.VMEM((near_rows + WINDOW, 2 * width), BF16),
            pltpu.VMEM((tiles, 2 * TILE, width), BF16),
            pltpu.VMEM((CHUNK, 2 * width), F32),
            pltpu.VMEM((CHUNK, 2 * width), F32),
        ),
        smem=(0, 1),
        cost=14,
    )
    halos, near_totals, expert_in, expert_out = hold((halos, near_totals, expert_in, expert_out))
    for s in range(1, narrow_count):
        if s not in EARLY_IN:
            in_blocks[s] = around(weight_to(expert_in, s), s)
        out_blocks[s] = around(weight_to(expert_out, s), s)
    graph_out, weight_first, send = call(
        far_kernel,
        (
            array((rows, width), BF16),
            array((rows, 1), F32),
            array((experts, PANELS * capacity, 128), BF16),
        ),
        (
            keys,
            near_count,
            key_col,
            key_row,
            *halos[1:],
            source_weight,
            near_totals,
            dest,
            node_feats,
            norm_gain.reshape(1, width),
            router_weight,
            routes,
            slot_row,
            cotangent,
        ),
        scratch=(
            pltpu.VMEM((3 * per_narrow + WINDOW, 2 * width), BF16),
            pltpu.VMEM((tiles, 2 * TILE, width), BF16),
            pltpu.VMEM((CHUNK, 2 * width), F32),
            pltpu.VMEM((CHUNK, 2 * width), F32),
            pltpu.VMEM((tiles, TILE, 2 * width), F32),
        ),
        smem=(0, 1),
        cost=18,
    )
    sooner = [in_blocks[s] for s in SOON_IN] + [out_blocks[s] for s in SOON_OUT]
    send, sooner = hold((send, sooner))
    for s, block in zip(SOON_IN, sooner):
        in_blocks[s] = block
    for s, block in zip(SOON_OUT, sooner[len(SOON_IN) :]):
        out_blocks[s] = block
    arrived = lax.all_to_all(send, OWNERS, split_axis=0, concat_axis=0, tiled=True)
    blocks = in_blocks + out_blocks
    hidden_block = expert_in.shape[2]
    expert = (lax.axis_index("wide") * 2 + my_lo).astype(I32).reshape(1)
    saved = array((4, experts * capacity, hidden_block), BF16)
    back, router_part, act_all, hidden_all = call(
        expert_kernel,
        (
            array((experts, 2, capacity, width), BF16),
            array((experts, width), F32),
            saved,
            saved,
        ),
        (expert, arrived, *blocks),
        scratch=(pltpu.VMEM((experts, width), F32),),
        smem=(0,),
        cost=12,
    )
    router_part = router_part.astype(BF16)
    twin = lax.ppermute(router_part, "wide", [(i, i ^ 1) for i in range(wide_count)])
    router_sum = router_part.astype(F32) + twin.astype(F32)
    back = lax.all_to_all(
        back.reshape(experts, 2 * capacity, width), OWNERS, split_axis=0, concat_axis=0, tiled=True
    ).reshape(experts, 2, capacity, width)
    grad_shapes = [array((width, hidden_block), BF16)] * 4 + [array((hidden_block, width), BF16)] * 4
    grad_blocks = call(weight_kernel, grad_shapes, (arrived, act_all, hidden_all), cost=5)

    def sent_home(grads):
        return [grads[0]] + [around(grads[s], -s) for s in range(1, narrow_count)]

    def home(back):
        mine = back[0].astype(F32) + back[2].astype(F32)
        other = back[1].astype(F32) + back[3].astype(F32)
        low = my_lo == 0
        return jnp.stack([jnp.where(low, mine, other), jnp.where(low, other, mine)])

    in_back = sent_home(grad_blocks[:4])
    out_back = sent_home(grad_blocks[4:])
    router_sum = add_axis(router_sum, NARROW, lambda s: ring(narrow_count, s))
    router_sum, back, in_back, out_back[1] = hold((router_sum, back, in_back, out_back[1]))
    router_sum = add_axis(router_sum, "wide", lambda s: along(wide_count, 2, s))
    router_sum, out_back = hold((router_sum, out_back))
    router_total = add_axis(router_sum, "wide", lambda s: along(wide_count, 8, s))
    layer_out, grad_features = call(
        output_kernel,
        (array((rows, width), BF16), array((rows, width), F32)),
        (back, slot_col, graph_out, weight_first, cotangent, routes, router_weight.T),
        cost=5,
    )
    grad_expert_in = home(in_back)
    grad_expert_out = home(out_back)
    grad_router = router_total.T
    return (layer_out, grad_features, grad_expert_in, grad_expert_out, grad_router)


def solution(mesh):
    wide_count, narrow_count = mesh.devices.shape
    fine = Mesh(mesh.devices.reshape(wide_count, narrow_count // 2, 2), ALL)
    placed = (
        P(ALL, None),
        P("wide", NARROW, None, None),
        P(ALL, None),
        P(ALL, None),
        P(),
        P(),
        P(),
        P(),
        P(ALL, None),
        P("wide", None, NARROW),
        P("wide", NARROW, None),
        P(ALL, None),
    )
    return jax.shard_map(
        on_device,
        mesh=fine,
        in_specs=placed,
        out_specs=(
            P(ALL, None),
            P(ALL, None),
            P("wide", None, NARROW),
            P("wide", NARROW, None),
            P(),
        ),
        check_vma=False,
    )
```
